32 devices in a mesh: groups: 2 (over x), ctx: 16 (over z, y, core).
Axes of the slice: x: 2, y: 2, z: 4, core: 2. Of those that a mesh axis runs over, the one named last changes fastest.
Arguments:
- queries: bfloat16 [2048, 2048], P('ctx', 'groups'), parts along dimension 1, may hold values from -25 to 25
- keys: bfloat16 [2048, 256], P('ctx', 'groups'), parts along dimension 1, may hold values from -6 to 6
- values: bfloat16 [2048, 256], P('ctx', 'groups'), parts along dimension 1, may hold values from -6 to 6
- d_out: bfloat16 [2048, 2048], P('ctx', 'groups'), parts along dimension 1, may hold values from -96 to 96
- mixer_input: bfloat16 [2048, 4096], P('ctx', 'groups'), parts along dimension 1, may hold values from -54 to 54
- gate_input: bfloat16 [2048, 4096], P('ctx', 'groups'), parts along dimension 1, may hold values from -6 to 6
- state_write: bfloat16 [2048, 512], P('ctx', 'groups'), parts along dimension 1, may hold values from -0.375 to 0.375
- state_read: bfloat16 [2048, 512], P('ctx', 'groups'), parts along dimension 1, may hold values from -0.375 to 0.375
- log_decay: float32 [2048, 64], P('ctx', 'groups'), parts along dimension 1, may hold values from -1 to 0
- norm_gain: float32 [4096], P('groups'), parts along dimension 0, may hold values from 0.25 to 1.75
- project_weight: bfloat16 [2048, 2560], P(None, 'groups'), parts along dimension 1, may hold values from -0.125 to 0.125
Outputs:
- input_gradient: float32 [2048, 4096], P('ctx', 'groups'), parts along dimension 1
- gate_gradient: float32 [2048, 4096], P('ctx', 'groups'), parts along dimension 1
- write_gradient: float32 [2048, 512], P('ctx', 'groups'), parts along dimension 1
- read_gradient: float32 [2048, 512], P('ctx', 'groups'), parts along dimension 1
The draws below stay inside these ranges and needn't reach their ends.
There are 2 independent parts, one for each index of `groups`. The reference program is written for one: setup_inputs(seed, part) draws one part's arguments, and reference() takes and returns one part's arrays. A program takes and returns all parts, laid end to end along the dimension named above; each array names one. Nothing has to cross between parts.
All inputs are finite; a program needn't handle non-finite values.
Results may differ from the reference program's by a relative error of at most 0.011.
Values may be sent and summed in bfloat16 or wider, within the bound.
A program may use at most 192 MiB of HBM per device.

```python
import math
import jax
import jax.numpy as jnp
from jax import lax

TOK_DEV = 128
HEADS = 8
HEAD_DIM = 128
MHEADS = 32
MDIM = 64
NSTATE = 256
STRIDE = 16
WINDOW_TOKENS = 2048
CHANNELS = 2048
PROJECT = 1280


def draw_queries(key, part):
    value_key = jax.random.fold_in(key, 7002)
    base = jnp.clip(jax.random.normal(value_key, (WINDOW_TOKENS, HEADS * HEAD_DIM), jnp.float32), -6.0, 6.0)
    return base.astype(jnp.bfloat16)


def draw_keys(key, part):
    value_key = jax.random.fold_in(key, 7003)
    base = jnp.clip(jax.random.normal(value_key, (WINDOW_TOKENS, HEAD_DIM), jnp.float32), -6.0, 6.0)
    return base.astype(jnp.bfloat16)


def draw_mixer_input(key, part):
    row_key = jax.random.fold_in(key, 7101)
    column_key = jax.random.fold_in(key, 7102)
    value_key = jax.random.fold_in(key, 7103)
    row_scale = jnp.exp(jax.random.uniform(row_key, (WINDOW_TOKENS,), jnp.float32, minval=math.log(0.3), maxval=math.log(3.0)))
    base = jnp.clip(jax.random.normal(value_key, (WINDOW_TOKENS, CHANNELS), jnp.float32), -6.0, 6.0)
    column_scale = jnp.exp(jax.random.uniform(column_key, (CHANNELS,), jnp.float32, minval=math.log(0.3), maxval=math.log(3.0)))
    return (base * row_scale[:, None] * column_scale[None, :]).astype(jnp.bfloat16)


def draw_log_decay(key, part):
    pick_key = jax.random.fold_in(key, 7201)
    forgetful = jax.random.randint(pick_key, (MHEADS,), 0, 2) == 1
    fast_rate = jnp.exp(jax.random.uniform(jax.random.fold_in(key, 7202), (MHEADS,), jnp.float32, minval=math.log(1.0 / 50.0), maxval=math.log(1.0 / 30.0)))
    slow_rate = jnp.exp(jax.random.uniform(jax.random.fold_in(key, 7203), (MHEADS,), jnp.float32, minval=math.log(0.1), maxval=math.log(0.5))) / WINDOW_TOKENS
    head_rate = jnp.where(forgetful, fast_rate, slow_rate)
    device_factor = jnp.exp(jax.random.uniform(jax.random.fold_in(key, 7204), (STRIDE,), jnp.float32, minval=math.log(0.5), maxval=math.log(2.0)))
    every_row = jnp.arange(WINDOW_TOKENS)
    row_factor = device_factor[every_row // TOK_DEV]
    token_factor = jax.random.uniform(jax.random.fold_in(key, 7205), (WINDOW_TOKENS, MHEADS), jnp.float32, minval=0.5, maxval=1.5)
    decay_factor = -head_rate[None, :] * row_factor[:, None] * token_factor
    group_rows = jax.random.randint(jax.random.fold_in(key, 7206), (2,), 0, WINDOW_TOKENS)
    group_depth = jax.random.uniform(jax.random.fold_in(key, 7207), (2,), jnp.float32, minval=math.log(0.5), maxval=math.log(0.8))
    row_groups = jnp.sum(jnp.where(every_row[:, None] == group_rows[None, :], group_depth[None, :], 0.0), axis=1)
    return decay_factor + row_groups[:, None]


def shard_levels(stream_key, dims, pieces, smallest, top_value):
    def one(dim, parts):
        draws = jax.random.uniform(jax.random.fold_in(jax.random.fold_in(stream_key, 6), dim), (parts,), jnp.float32, smallest / len(pieces), top_value / len(pieces))
        return jnp.repeat(jnp.exp(draws), dims[dim] // parts).reshape((-1,) + (1,) * (len(dims) - dim - 1))

    factor_of = one(*pieces[0])
    for cut in pieces[1:]:
        factor_of = factor_of * one(*cut)
    return factor_of


def scatter_about(rng, shape, scale, bound, pieces=(), held_as=jnp.bfloat16):
    level = shard_levels(rng, shape, pieces, -0.22, 0.18) if pieces else 1.0
    array = jax.random.normal(rng, shape, jnp.float32) * scale * level
    return jnp.minimum(jnp.maximum(array, -bound), bound).astype(held_as)


def setup_inputs(seed: int = 0, part: int = 0) -> dict:
    seeds = jax.random.split(jax.random.key(seed), 12)
    own_keys = jax.random.split(jax.random.fold_in(seeds[11], part), 12)
    return {
        "queries": draw_queries(jax.random.fold_in(jax.random.fold_in(seeds[11], part), 71), part),
        "keys": draw_keys(jax.random.fold_in(jax.random.fold_in(seeds[11], part), 71), part),
        "values": scatter_about(own_keys[2], (WINDOW_TOKENS, HEAD_DIM), 1.0, 6.0, ((0, 16),)),
        "d_out": scatter_about(own_keys[3], (WINDOW_TOKENS, HEADS * HEAD_DIM), 16.0, 96.0, ((0, 16),)),
        "mixer_input": draw_mixer_input(jax.random.fold_in(jax.random.fold_in(seeds[11], part), 71), part),
        "gate_input": scatter_about(own_keys[5], (WINDOW_TOKENS, CHANNELS), 1.0, 6.0, ((0, 16),)),
        "state_write": scatter_about(own_keys[6], (WINDOW_TOKENS, NSTATE), NSTATE ** -0.5, 0.375, ((0, 16),)),
        "state_read": scatter_about(own_keys[7], (WINDOW_TOKENS, NSTATE), NSTATE ** -0.5, 0.375, ((0, 16),)),
        "log_decay": draw_log_decay(jax.random.fold_in(jax.random.fold_in(seeds[11], part), 71), part),
        "norm_gain": jnp.clip(1.0 + 0.15 * jax.random.normal(own_keys[9], (CHANNELS,), jnp.float32), 0.25, 1.75),
        "project_weight": scatter_about(own_keys[10], (CHANNELS, PROJECT), CHANNELS ** -0.5, 0.125),
    }


EPSILON = 1e-05
HIGHEST = lax.Precision.HIGHEST

def decay_parts(log_decay):
    cumulated = jnp.cumsum(log_decay, axis=0)
    length = cumulated.shape[0]
    causal_mask = (jnp.arange(length)[:, None] >= jnp.arange(length)[None, :])[None, :, :]
    spread = cumulated.T[:, :, None] - cumulated.T[:, None, :]
    decays = jnp.where(causal_mask, jnp.exp(jnp.where(causal_mask, spread, 0.0)), 0.0)
    remaining = jnp.exp(cumulated[-1][None, :] - cumulated)
    return (cumulated, decays, remaining)

def local_state(values_f, write_f, remaining):
    return jnp.einsum('shp,sn->hpn', values_f * remaining[:, :, None], write_f, precision=HIGHEST)

def block_output(weights, values_f, read_f, cumulated, incoming):
    within = jnp.einsum('hts,shp->thp', weights, values_f, precision=HIGHEST)
    carried = jnp.einsum('hpn,tn->thp', incoming, read_f, precision=HIGHEST)
    return within + jnp.exp(cumulated)[:, :, None] * carried

def local_adjoint(grads_f, read_f, cumulated):
    return jnp.einsum('thp,tn->hpn', grads_f * jnp.exp(cumulated)[:, :, None], read_f, precision=HIGHEST)

def block_grads(weights, decays, values_f, grads_f, write_f, read_f, cumulated, remaining, incoming, adjoint):
    value_grad = jnp.einsum('hts,thp->shp', weights, grads_f, precision=HIGHEST)
    value_grad = value_grad + remaining[:, :, None] * jnp.einsum('hpn,sn->shp', adjoint, write_f, precision=HIGHEST)
    pairs = jnp.einsum('thp,shp->hts', grads_f, values_f, precision=HIGHEST)
    pair_sum = lax.optimization_barrier(jnp.sum(decays * pairs, axis=0))
    read_grad = jnp.dot(pair_sum, write_f, precision=HIGHEST) + jnp.einsum('thp,hpn->tn', grads_f * jnp.exp(cumulated)[:, :, None], incoming, precision=HIGHEST)
    write_grad = jnp.dot(pair_sum.T, read_f, precision=HIGHEST) + jnp.einsum('shp,hpn->sn', values_f * remaining[:, :, None], adjoint, precision=HIGHEST)
    return (value_grad, write_grad, read_grad)

def gate_grads(mixer_out, gate_input, norm_gain, mixer_grad):
    gate_f = gate_input.astype(jnp.float32)
    sigmoid = jax.nn.sigmoid(gate_f)
    active = gate_f * sigmoid
    gated = mixer_out * active
    root_mean = jnp.sqrt(lax.optimization_barrier(jnp.mean(gated * gated, axis=-1, keepdims=True)) + EPSILON)
    scaled = norm_gain[None, :] * mixer_grad.astype(jnp.float32)
    gated_grad = scaled / root_mean - gated * lax.optimization_barrier(jnp.mean(scaled * gated, axis=-1, keepdims=True)) / root_mean ** 3
    gate_gradient = gated_grad * mixer_out * sigmoid * (1.0 + gate_f * (1.0 - sigmoid))
    out_grad = (gated_grad * active).astype(jnp.bfloat16)
    return (out_grad, gate_gradient)

def reference(queries, keys, values, d_out, mixer_input, gate_input, state_write, state_read, log_decay, norm_gain, project_weight):
    scale = 1.0 / math.sqrt(HEAD_DIM)
    every_row = jnp.arange(WINDOW_TOKENS, dtype=jnp.int32)
    position = every_row % TOK_DEV * STRIDE + every_row // TOK_DEV
    query_f = queries.astype(jnp.float32).reshape(WINDOW_TOKENS, HEADS, HEAD_DIM)
    grad_f = d_out.astype(jnp.float32).reshape(WINDOW_TOKENS, HEADS, HEAD_DIM)
    keys_f = keys.astype(jnp.float32)
    values_f = values.astype(jnp.float32)
    width = math.gcd(WINDOW_TOKENS, 512)
    count = WINDOW_TOKENS // width

    def query_block(carry, block_index):
        key_acc, value_acc = carry
        start = (block_index * width).astype(jnp.int32)
        query_part = lax.dynamic_slice_in_dim(query_f, start, width, 0)
        grad_part = lax.dynamic_slice_in_dim(grad_f, start, width, 0)
        place_part = lax.dynamic_slice_in_dim(position, start, width, 0)
        raw_scores = jnp.einsum('qhe,ke->qhk', query_part, keys_f) * scale
        visible = place_part[:, None, None] >= position[None, None, :]
        masked = jnp.where(visible, raw_scores, -jnp.inf)
        highest_score = lax.optimization_barrier(jnp.max(masked, axis=-1, keepdims=True))
        log_total = highest_score + jnp.log(lax.optimization_barrier(jnp.sum(jnp.exp(masked - highest_score), axis=-1, keepdims=True)))
        probs_f = jnp.exp(masked - log_total)
        probs_low = lax.optimization_barrier(probs_f.astype(jnp.bfloat16)).astype(jnp.float32)
        attention_out = jnp.einsum('qhk,kd->qhd', probs_low, values_f)
        delta = lax.optimization_barrier(jnp.sum(grad_part * attention_out, axis=-1, keepdims=True))
        prob_grad = jnp.einsum('qhd,kd->qhk', grad_part, values_f)
        score_grad = lax.optimization_barrier((probs_f * (prob_grad - delta)).astype(jnp.bfloat16)).astype(jnp.float32)
        query_grad = (jnp.einsum('qhk,ke->qhe', score_grad, keys_f) * scale).astype(jnp.bfloat16)
        key_acc = key_acc + jnp.einsum('qhk,qhe->ke', score_grad, query_part) * scale
        value_acc = value_acc + jnp.einsum('qhk,qhd->kd', probs_low, grad_part)
        return ((key_acc, value_acc), query_grad)
    empty_rows = jnp.zeros((WINDOW_TOKENS, HEAD_DIM), jnp.float32)
    (key_acc, value_acc), query_grads = lax.scan(query_block, (empty_rows, empty_rows), jnp.arange(count, dtype=jnp.int32))
    query_grads = query_grads.reshape(WINDOW_TOKENS, HEADS * HEAD_DIM)
    all_grads = jnp.concatenate([query_grads, key_acc.astype(jnp.bfloat16), value_acc.astype(jnp.bfloat16)], axis=1)
    attention_grad = jnp.dot(all_grads, project_weight.T, preferred_element_type=jnp.float32).astype(jnp.bfloat16)
    mixer_grad = attention_grad.reshape(STRIDE, TOK_DEV, CHANNELS).transpose(1, 0, 2).reshape(WINDOW_TOKENS, CHANNELS)
    input_blocks = mixer_input.reshape(STRIDE, TOK_DEV, CHANNELS)
    write_blocks = state_write.reshape(STRIDE, TOK_DEV, NSTATE)
    read_blocks = state_read.reshape(STRIDE, TOK_DEV, NSTATE)
    decay_blocks = log_decay.reshape(STRIDE, TOK_DEV, MHEADS)

    def forward_block(incoming, block):
        inputs_part, write_part, read_part, decay_part = block
        values_part = inputs_part.astype(jnp.float32).reshape(TOK_DEV, MHEADS, MDIM)
        write_f = write_part.astype(jnp.float32)
        read_f = read_part.astype(jnp.float32)
        cumulated, decays, remaining = decay_parts(decay_part)
        products = jnp.dot(read_part, write_part.T, preferred_element_type=jnp.float32)
        weights = decays * products[None, :, :]
        output = block_output(weights, values_part, read_f, cumulated, incoming)
        outgoing = jnp.exp(cumulated[-1])[:, None, None] * incoming + local_state(values_part, write_f, remaining)
        return (outgoing, (output.reshape(TOK_DEV, CHANNELS), incoming))
    start_state = jnp.zeros((MHEADS, MDIM, NSTATE), jnp.float32)
    _, (outputs, incomings) = lax.scan(forward_block, start_state, (input_blocks, write_blocks, read_blocks, decay_blocks))
    mixer_out = outputs.reshape(WINDOW_TOKENS, CHANNELS)
    out_grad, gate_gradient = gate_grads(mixer_out, gate_input, norm_gain, mixer_grad)

    def backward_block(adjoint, block):
        inputs_part, write_part, read_part, decay_part, grad_part, incoming = block
        values_part = inputs_part.astype(jnp.float32).reshape(TOK_DEV, MHEADS, MDIM)
        grads_part = grad_part.astype(jnp.float32).reshape(TOK_DEV, MHEADS, MDIM)
        write_f = write_part.astype(jnp.float32)
        read_f = read_part.astype(jnp.float32)
        cumulated, decays, remaining = decay_parts(decay_part)
        products = jnp.dot(read_part, write_part.T, preferred_element_type=jnp.float32)
        weights = decays * products[None, :, :]
        value_grad, write_grad, read_grad = block_grads(weights, decays, values_part, grads_part, write_f, read_f, cumulated, remaining, incoming, adjoint)
        outgoing = jnp.exp(cumulated[-1])[:, None, None] * adjoint + local_adjoint(grads_part, read_f, cumulated)
        return (outgoing, (value_grad.reshape(TOK_DEV, CHANNELS), write_grad, read_grad))
    grad_blocks = out_grad.reshape(STRIDE, TOK_DEV, CHANNELS)
    _, (value_grads, write_grads, read_grads) = lax.scan(backward_block, start_state, (input_blocks, write_blocks, read_blocks, decay_blocks, grad_blocks, incomings), reverse=True)
    return (value_grads.reshape(WINDOW_TOKENS, CHANNELS), gate_gradient, write_grads.reshape(WINDOW_TOKENS, NSTATE), read_grads.reshape(WINDOW_TOKENS, NSTATE))
```

```python
import functools
import math

import jax
import jax.numpy as jnp
from jax import lax
from jax.experimental import pallas as pl
from jax.experimental.pallas import tpu as pltpu
from jax.sharding import PartitionSpec as P

EPSILON = 1e-05
HIGHEST = lax.Precision.HIGHEST


def carried_in(part, axis, combine, identity, reverse):
    count = lax.axis_size(axis)
    place = lax.axis_index(axis)
    ahead = count - 1 - place if reverse else place
    gathered = jax.tree.map(lambda a: lax.all_gather(a, axis), part)
    state = jax.tree.map(lambda a, e: jnp.zeros_like(a) + jnp.asarray(e, a.dtype), part, identity)

    def one(hop, state):
        source = count - 1 - hop if reverse else hop
        return combine(
            state, jax.tree.map(lambda a: lax.dynamic_index_in_dim(a, source, 0, False), gathered)
        )

    return lax.fori_loop(0, ahead, one, state)


def decay_parts(log_decay):
    length = log_decay.shape[0]
    lower = jnp.tril(jnp.ones((length, length), jnp.float32))
    cumulated = jnp.dot(lower, log_decay, precision=HIGHEST)
    causal_mask = (jnp.arange(length)[:, None] >= jnp.arange(length)[None, :])[None, :, :]
    spread = cumulated.T[:, :, None] - cumulated.T[:, None, :]
    decays = jnp.where(causal_mask, jnp.exp(jnp.where(causal_mask, spread, 0.0)), 0.0)
    remaining = jnp.exp(cumulated[-1][None, :] - cumulated)
    return (cumulated, decays, remaining)


def local_state(values_f, write_f, remaining):
    return jnp.einsum("shp,sn->hpn", values_f * remaining[:, :, None], write_f, precision=HIGHEST)


def block_output(weights, values_f, read_f, cumulated, incoming):
    within = jnp.einsum("hts,shp->thp", weights, values_f, precision=HIGHEST)
    carried = jnp.einsum("hpn,tn->thp", incoming, read_f, precision=HIGHEST)
    return within + jnp.exp(cumulated)[:, :, None] * carried


def local_adjoint(grads_f, read_f, cumulated):
    return jnp.einsum(
        "thp,tn->hpn", grads_f * jnp.exp(cumulated)[:, :, None], read_f, precision=HIGHEST
    )


def block_grads(
    weights, decays, values_f, grads_f, write_f, read_f, cumulated, remaining, incoming, adjoint
):
    value_grad = jnp.einsum("hts,thp->shp", weights, grads_f, precision=HIGHEST)
    value_grad = value_grad + remaining[:, :, None] * jnp.einsum(
        "hpn,sn->shp", adjoint, write_f, precision=HIGHEST
    )
    pairs = jnp.einsum("thp,shp->hts", grads_f, values_f, precision=HIGHEST)
    pair_sum = jnp.sum(decays * pairs, axis=0)
    read_grad = jnp.dot(pair_sum, write_f, precision=HIGHEST) + jnp.einsum(
        "thp,hpn->tn", grads_f * jnp.exp(cumulated)[:, :, None], incoming, precision=HIGHEST
    )
    write_grad = jnp.dot(pair_sum.T, read_f, precision=HIGHEST) + jnp.einsum(
        "shp,hpn->sn", values_f * remaining[:, :, None], adjoint, precision=HIGHEST
    )
    return (value_grad, write_grad, read_grad)


def gate_grads(mixer_out, gate_input, norm_gain, mixer_grad):
    gate_f = gate_input.astype(jnp.float32)
    sigmoid = jax.nn.sigmoid(gate_f)
    active = gate_f * sigmoid
    gated = mixer_out * active
    root_mean = jnp.sqrt(jnp.mean(gated * gated, axis=-1, keepdims=True) + EPSILON)
    scaled = norm_gain[None, :] * mixer_grad.astype(jnp.float32)
    gated_grad = (
        scaled / root_mean - gated * jnp.mean(scaled * gated, axis=-1, keepdims=True) / root_mean**3
    )
    gate_gradient = gated_grad * mixer_out * sigmoid * (1.0 + gate_f * (1.0 - sigmoid))
    out_grad = (gated_grad * active).astype(jnp.bfloat16)
    return (out_grad, gate_gradient)


def compose(earlier, later):
    return (earlier[0] * later[0], later[0][:, None, None] * earlier[1] + later[1])


def token_order(received, ctx_size, rows):
    per_partner = rows // ctx_size
    return received.reshape(ctx_size, per_partner, -1).transpose(1, 0, 2).reshape(rows, -1)


def apply_weight(grad_rows, project_weight):
    return lax.dot_general(
        grad_rows, project_weight, (((1,), (1,)), ((), ())), preferred_element_type=jnp.float32
    ).astype(jnp.bfloat16)


def body(
    queries,
    keys,
    values,
    d_out,
    mixer_input,
    gate_input,
    state_write,
    state_read,
    log_decay,
    norm_gain,
    project_weight,
):
    ctx_size = lax.axis_size("ctx")
    ctx_index = lax.axis_index("ctx")
    rows = keys.shape[0]
    head_dim = keys.shape[1]
    heads = queries.shape[1] // head_dim
    scale = 1.0 / math.sqrt(head_dim)
    query_heads = queries.reshape(rows, heads, head_dim)
    grad_heads = d_out.reshape(rows, heads, head_dim)
    query_pos = jnp.arange(rows, dtype=jnp.int32) * ctx_size + ctx_index
    mheads = log_decay.shape[1]
    channels = mixer_input.shape[1]
    mdim = channels // mheads
    values_f = mixer_input.astype(jnp.float32).reshape(rows, mheads, mdim)
    write_f = state_write.astype(jnp.float32)
    read_f = state_read.astype(jnp.float32)
    cumulated, decays, remaining = decay_parts(log_decay)
    products = jnp.dot(state_read, state_write.T, preferred_element_type=jnp.float32)
    weights = decays * products[None, :, :]
    own_state = local_state(values_f, write_f, remaining)
    passing = jnp.exp(cumulated[-1])
    identity = (jnp.ones_like(passing), jnp.zeros_like(own_state))
    _, incoming = carried_in((passing, own_state), "ctx", compose, identity, False)
    all_keys, all_values = (
        lax.all_gather(keys, "ctx", axis=0, tiled=True),
        lax.all_gather(values, "ctx", axis=0, tiled=True),
    )
    total = all_keys.shape[0]
    total_rows = jnp.arange(total, dtype=jnp.int32)
    key_pos = total_rows % rows * ctx_size + total_rows // rows
    width = math.gcd(total, 512)
    count = total // width
    key_blocks = all_keys.reshape(count, width, head_dim)
    value_blocks = all_values.reshape(count, width, head_dim)
    place_blocks = key_pos.reshape(count, width)

    def scores_of(key_block, place_block):
        raw_scores = (
            jnp.einsum("qhe,ke->qhk", query_heads, key_block, preferred_element_type=jnp.float32)
            * scale
        )
        visible = query_pos[:, None, None] >= place_block[None, None, :]
        return jnp.where(visible, raw_scores, -jnp.inf)

    def total_step(carry, block):
        running_max, running_sum = carry
        masked = scores_of(block[0], block[1])
        new_max = jnp.maximum(running_max, jnp.max(masked, axis=-1))
        running_sum = running_sum * jnp.exp(running_max - new_max) + jnp.sum(
            jnp.exp(masked - new_max[:, :, None]), axis=-1
        )
        return ((new_max, running_sum), None)

    start_max = jnp.full((rows, heads), -1e30, jnp.float32)
    start_sum = jnp.zeros((rows, heads), jnp.float32)
    (final_max, final_sum), _ = lax.scan(
        total_step, (start_max, start_sum), (key_blocks, place_blocks)
    )
    log_total = final_max + jnp.log(final_sum)

    def output_step(carry, block):
        masked = scores_of(block[0], block[1])
        probs_low = jnp.exp(masked - log_total[:, :, None]).astype(jnp.bfloat16)
        return (
            carry
            + jnp.einsum("qhk,kd->qhd", probs_low, block[2], preferred_element_type=jnp.float32),
            None,
        )

    attention_out, _ = lax.scan(
        output_step,
        jnp.zeros((rows, heads, head_dim), jnp.float32),
        (key_blocks, place_blocks, value_blocks),
    )
    delta = jnp.sum(grad_heads.astype(jnp.float32) * attention_out, axis=-1)

    def score_parts(block):
        masked = scores_of(block[0], block[1])
        probs_f = jnp.exp(masked - log_total[:, :, None])
        prob_grad = jnp.einsum(
            "qhd,kd->qhk", grad_heads, block[2], preferred_element_type=jnp.float32
        )
        score_grad = (probs_f * (prob_grad - delta[:, :, None])).astype(jnp.bfloat16)
        return (probs_f.astype(jnp.bfloat16), score_grad)

    start_query = jnp.zeros((rows, heads, head_dim), jnp.float32)

    def query_step(carry, block):
        probs_low, score_grad = score_parts(block)
        return (
            carry
            + jnp.einsum("qhk,ke->qhe", score_grad, block[0], preferred_element_type=jnp.float32),
            None,
        )

    query_acc, _ = lax.scan(query_step, start_query, (key_blocks, place_blocks, value_blocks))
    all_queries, all_grads = (
        lax.all_gather(queries, "ctx", axis=0, tiled=True),
        lax.all_gather(d_out, "ctx", axis=0, tiled=True),
    )
    all_totals, all_deltas = (
        lax.all_gather(log_total, "ctx", axis=0, tiled=True),
        lax.all_gather(delta, "ctx", axis=0, tiled=True),
    )
    query_blocks = all_queries.reshape(count, width, heads, head_dim)
    grad_blocks = all_grads.reshape(count, width, heads, head_dim)
    total_blocks = all_totals.reshape(count, width, heads)
    delta_blocks = all_deltas.reshape(count, width, heads)

    def key_step(carry, block):
        key_acc, value_acc = carry
        query_block, grad_block, total_block, delta_block, place_block = block
        raw_scores = (
            jnp.einsum("qhe,ke->qhk", query_block, keys, preferred_element_type=jnp.float32) * scale
        )
        visible = place_block[:, None, None] >= query_pos[None, None, :]
        masked = jnp.where(visible, raw_scores, -jnp.inf)
        probs_f = jnp.exp(masked - total_block[:, :, None])
        probs_low = probs_f.astype(jnp.bfloat16)
        prob_grad = jnp.einsum(
            "qhd,kd->qhk", grad_block, values, preferred_element_type=jnp.float32
        )
        score_grad = (probs_f * (prob_grad - delta_block[:, :, None])).astype(jnp.bfloat16)
        key_acc = (
            key_acc
            + jnp.einsum("qhk,qhe->ke", score_grad, query_block, preferred_element_type=jnp.float32)
            * scale
        )
        value_acc = value_acc + jnp.einsum(
            "qhk,qhd->kd", probs_low, grad_block, preferred_element_type=jnp.float32
        )
        return ((key_acc, value_acc), None)

    empty_keys = jnp.zeros((rows, head_dim), jnp.float32)
    (key_acc, value_acc), _ = lax.scan(
        key_step,
        (empty_keys, empty_keys),
        (query_blocks, grad_blocks, total_blocks, delta_blocks, place_blocks),
    )
    key_grad = key_acc.astype(jnp.bfloat16)
    value_grad = value_acc.astype(jnp.bfloat16)
    query_grad = (query_acc * scale).astype(jnp.bfloat16).reshape(rows, heads * head_dim)
    projected = jnp.concatenate([query_grad, key_grad, value_grad], axis=1)
    mixed = apply_weight(projected, project_weight)
    mixer_grad = token_order(
        lax.all_to_all(mixed, "ctx", split_axis=0, concat_axis=0, tiled=True), ctx_size, rows
    )
    mixer_out = block_output(weights, values_f, read_f, cumulated, incoming).reshape(rows, channels)
    out_grad, gate_gradient = gate_grads(mixer_out, gate_input, norm_gain, mixer_grad)
    grads_f = out_grad.astype(jnp.float32).reshape(rows, mheads, mdim)
    own_adjoint = local_adjoint(grads_f, read_f, cumulated)
    _, adjoint = carried_in((passing, own_adjoint), "ctx", compose, identity, True)
    input_grad, write_gradient, read_gradient = block_grads(
        weights, decays, values_f, grads_f, write_f, read_f, cumulated, remaining, incoming, adjoint
    )
    return (input_grad.reshape(rows, channels), gate_gradient, write_gradient, read_gradient)


F32 = jnp.float32
BF16 = jnp.bfloat16
MESH = pl.DeviceIdType.MESH
LANES = 128
(
    KEY_OUTER,
    KEY_CHIP,
    KEY_CORE,
    VALUE_OUTER,
    VALUE_CHIP,
    VALUE_CORE,
    TOTAL,
    QUERY_ROWS,
    GRAD_CORE,
    GRAD_CHIP,
    GRAD_OUTER,
) = range(11)
FORWARD = 11
BACKWARD = 16
PHASES = 21
PLANE = 4


def dot(a, b, dims):
    return lax.dot_general(a, b, (dims, ((), ())), preferred_element_type=F32)


NN = ((1,), (0,))
NT = ((1,), (1,))
TN = ((0,), (0,))


def fused_kernel(
    size,
    mdim,
    q_hbm,
    k_hbm,
    v_hbm,
    do_hbm,
    x_hbm,
    gate_hbm,
    write_hbm,
    read_hbm,
    decay_hbm,
    gain_hbm,
    weight_hbm,
    igrad_ref,
    ggrad_ref,
    wgrad_ref,
    rgrad_ref,
    q_ref,
    do_ref,
    x_ref,
    gate_ref,
    write_ref,
    read_ref,
    decay_ref,
    gain_ref,
    cum_ref,
    kbuf,
    vbuf,
    own_totals,
    totals,
    rows_out,
    rows_in,
    keys_out,
    keys_core,
    keys_chip_out,
    keys_chip,
    keys_outer_out,
    keys_outer,
    states,
    states_core,
    states_chip_out,
    states_chip,
    states_outer_out,
    states_outer,
    incoming_chip_out,
    incoming_chip,
    incoming_out,
    incoming,
    adjoints,
    adjoints_core,
    adjoints_chip_out,
    adjoints_chip,
    adjoints_outer_out,
    adjoints_outer,
    returned_chip_out,
    returned_chip,
    returned_out,
    returned,
    exps,
    prob_grads,
    key_acc,
    value_acc,
    query_acc,
    decays,
    weights,
    grown,
    remain,
    mixer_out,
    mixed,
    out_grad,
    grown_grad,
    remain_input,
    pair_sum,
    weight,
    load_sem,
    ssem,
    rsem,
):
    me = lax.axis_index("ctx")
    _, rows, head_dim = kbuf.shape
    heads = q_ref.shape[1] // head_dim
    channels = x_ref.shape[1]
    per_piece = LANES // mdim
    blocks = key_acc.shape[0]
    width = rows // blocks
    per_partner = rows // size
    scale = 1.0 / math.sqrt(head_dim)

    outer = size // PLANE
    place = lax.rem(me, PLANE)
    core = lax.rem(me, 2)
    chip = place // 2
    far = me // PLANE
    core_peer = me + 1 - 2 * core
    chip_peer = me + 2 - 4 * chip
    nstate = write_ref.shape[1]

    def copy_to(src, dst, phase, sent_at, landed_at, peer):
        return pltpu.make_async_remote_copy(
            src_ref=src,
            dst_ref=dst,
            send_sem=ssem.at[phase, sent_at],
            recv_sem=rsem.at[phase, landed_at],
            device_id={"ctx": peer},
            device_id_type=MESH,
        )

    def arrived(dst, phase, at, peer):
        copy_to(dst, dst, phase, at, at, peer).wait_recv()

    def loop(first, last, fn):
        def one(step, carry):
            fn(step)
            return carry

        lax.fori_loop(first, last, one, 0)

    def each_peer(fn):
        def one(step, carry):
            fn(lax.rem(me + step, size))
            return carry

        lax.fori_loop(1, size, one, 0)

    def columns(piece):
        return pl.ds(pl.multiple_of(piece * LANES, LANES), LANES)

    loads = [
        pltpu.make_async_copy(source, target, load_sem.at[n])
        for n, (source, target) in enumerate(
            (
                (k_hbm, kbuf.at[me]),
                (v_hbm, vbuf.at[me]),
                (decay_hbm, decay_ref),
                (x_hbm, x_ref),
                (write_hbm, write_ref),
                (read_hbm, read_ref),
                (q_hbm, q_ref),
                (do_hbm, do_ref),
                (gain_hbm, gain_ref),
                (gate_hbm, gate_ref),
                (weight_hbm, weight),
            )
        )
    ]
    for load in loads:
        load.start()
    barrier = pltpu.get_barrier_semaphore()

    def greet(peer):
        pl.semaphore_signal(barrier, inc=1, device_id={"ctx": peer}, device_id_type=MESH)

    each_peer(greet)
    upper = (
        lax.broadcasted_iota(jnp.int32, (rows, rows), 0)
        <= lax.broadcasted_iota(jnp.int32, (rows, rows), 1)
    ).astype(F32)
    loads[2].wait()
    cum_ref[...] = lax.dot_general(
        decay_ref[...], upper, (NN, ((), ())), precision=HIGHEST, preferred_element_type=F32
    )
    loads[0].wait()
    loads[1].wait()
    pl.semaphore_wait(barrier, size - 1)

    def key_copies(phase_step, block, src_k, src_v, sent_at, peer):
        return (
            copy_to(src_k, kbuf.at[block], KEY_OUTER + phase_step, sent_at, block, peer),
            copy_to(src_v, vbuf.at[block], VALUE_OUTER + phase_step, sent_at, block, peer),
        )

    def start_keys(*arguments):
        for each in key_copies(*arguments):
            each.start()

    def far_device(step, at):
        return lax.rem(far + step, outer) * PLANE + at

    loop(
        1,
        outer,
        lambda step: start_keys(
            0, me, kbuf.at[me], vbuf.at[me], far_device(step, place), far_device(step, place)
        ),
    )
    start_keys(1, me, kbuf.at[me], vbuf.at[me], me, chip_peer)
    start_keys(2, me, kbuf.at[me], vbuf.at[me], me, core_peer)
    all_totals = jnp.broadcast_to(jnp.exp(cum_ref[:, rows - 1 : rows]), own_totals.shape)
    own_totals[...] = all_totals
    totals[place] = all_totals

    def total_copy(step):
        other = lax.rem(place + step, PLANE)
        return copy_to(
            own_totals, totals.at[place], TOTAL, other, place, far * PLANE + other
        )

    loop(1, PLANE, lambda step: total_copy(step).start())

    lane = lax.broadcasted_iota(jnp.int32, (rows, LANES), 1)
    row = lax.broadcasted_iota(jnp.int32, (rows, LANES), 0)
    lower = row >= lane

    half = 2 * outer

    def own_piece(piece):
        at = columns(piece)
        lines = [cum_ref[pl.ds(piece * per_piece + n, 1), :] for n in range(per_piece)]
        spread = jnp.concatenate(
            [jnp.broadcast_to(line, (mdim, rows)) for line in lines], axis=0
        ).T
        last = spread[rows - 1 : rows, :]
        left = jnp.exp(last - spread)
        grown[:, at] = jnp.exp(spread)
        remain[:, at] = left
        scaled_input = (x_ref[:, at].astype(F32) * left).astype(BF16)
        remain_input[:, at] = scaled_input
        states[piece] = dot(scaled_input, write_ref[...], TN).astype(BF16)

    def factor(source, piece):
        lines = [
            totals[source, pl.ds(piece * per_piece + n, 1), :] for n in range(per_piece)
        ]
        whole = jnp.concatenate(
            [jnp.broadcast_to(line, (mdim, LANES)) for line in lines], axis=0
        )
        return jnp.concatenate([whole] * (nstate // LANES), axis=1)

    def chip_factor(which, piece):
        return factor(2 * which, piece) * factor(2 * which + 1, piece)

    class Scan:
        def __init__(self, base, lead, buffers):
            self.base, self.lead = base, lead
            (
                self.own,
                self.core,
                self.chip_out,
                self.chip,
                self.outer_out,
                self.outer,
                self.back_chip_out,
                self.back_chip,
                self.back_out,
                self.result,
            ) = buffers

        def core_copy(self, piece):
            return copy_to(
                self.own.at[piece], self.core.at[piece], self.base, piece, piece, core_peer
            )

        def chip_copy(self, piece):
            return copy_to(
                self.chip_out.at[piece],
                self.chip.at[piece],
                self.base + 1,
                piece,
                piece,
                chip_peer,
            )

        def outer_copy(self, j):
            ahead = me - PLANE if self.lead else me + PLANE
            ahead = lax.rem(ahead + size, size)
            return copy_to(
                self.outer_out.at[j], self.outer.at[j], self.base + 2, j, j, ahead
            )

        def back_chip_copy(self, piece):
            return copy_to(
                self.back_chip_out.at[piece],
                self.back_chip.at[piece],
                self.base + 3,
                piece,
                piece,
                chip_peer,
            )

        def back_copy(self, piece):
            return copy_to(
                self.back_out.at[piece],
                self.result.at[piece],
                self.base + 4,
                piece,
                piece,
                core_peer,
            )

        def quarter(self, which, j):
            return (2 * core + which) * outer + j

        def core_states(self, piece):
            own = self.own[piece].astype(F32)
            other = self.core[piece].astype(F32)
            leads = core == self.lead
            return jnp.where(leads, own, other), jnp.where(leads, other, own)

        def core_source(self, which):
            return 2 * chip + which

        def join_cores(self, piece):
            arrived(self.core.at[piece], self.base, piece, core_peer)
            first, second = self.core_states(piece)
            later = factor(self.core_source(1 - self.lead), piece)
            self.chip_out[piece] = (later * first + second).astype(BF16)

        def join(self):
            def far_quarter(j):
                piece = self.quarter(1 - chip, j)
                self.join_cores(piece)
                self.chip_copy(piece).start()

            loop(0, outer, far_quarter)
            loop(0, outer, lambda j: self.join_cores(self.quarter(chip, j)))

        def chain(self):
            opens = far == (outer - 1 if self.lead else 0)
            closes = far == (0 if self.lead else outer - 1)
            leads = chip == self.lead

            def one(j):
                piece = self.quarter(chip, j)
                arrived(self.chip.at[piece], self.base + 1, piece, chip_peer)
                own = self.chip_out[piece].astype(F32)
                other = self.chip[piece].astype(F32)
                first = jnp.where(leads, own, other)
                second = jnp.where(leads, other, own)
                early = chip_factor(self.lead, piece)
                late = chip_factor(1 - self.lead, piece)

                @pl.when(opens)
                def _():
                    self.outer[j] = jnp.zeros((LANES, nstate), BF16)

                @pl.when(jnp.logical_not(opens))
                def _():
                    arrived(self.outer.at[j], self.base + 2, j, core_peer)

                state = self.outer[j].astype(F32)
                middle = early * state + first

                @pl.when(jnp.logical_not(closes))
                def _():
                    self.outer_out[j] = (late * middle + second).astype(BF16)
                    self.outer_copy(j).start()

                self.back_chip_out[piece] = jnp.where(leads, middle, state).astype(BF16)
                self.back_chip_copy(piece).start()
                self.back_chip[piece] = jnp.where(leads, state, middle).astype(BF16)

            loop(0, outer, one)

        def hand_back(self, piece):
            state = self.back_chip[piece].astype(F32)
            first, _ = self.core_states(piece)
            middle = factor(self.core_source(self.lead), piece) * state + first
            leads = core == self.lead
            self.back_out[piece] = jnp.where(leads, middle, state).astype(BF16)
            self.back_copy(piece).start()
            self.result[piece] = jnp.where(leads, state, middle).astype(BF16)

        def spread(self):
            loop(0, outer, lambda j: self.hand_back(self.quarter(chip, j)))

            def far_quarter(j):
                piece = self.quarter(1 - chip, j)
                arrived(self.back_chip.at[piece], self.base + 3, piece, chip_peer)
                self.hand_back(piece)

            loop(0, outer, far_quarter)

        def result_here(self, piece):
            @pl.when(piece // half != core)
            def _():
                arrived(self.result.at[piece], self.base + 4, piece, core_peer)

        def sent(self):
            closes = far == (0 if self.lead else outer - 1)

            def by_half(step):
                self.core_copy((1 - core) * half + step).wait_send()
                self.back_copy(core * half + step).wait_send()

            def by_quarter(j):
                self.chip_copy(self.quarter(1 - chip, j)).wait_send()
                self.back_chip_copy(self.quarter(chip, j)).wait_send()

                @pl.when(jnp.logical_not(closes))
                def _():
                    self.outer_copy(j).wait_send()

            loop(0, half, by_half)
            loop(0, outer, by_quarter)

    ahead_scan = Scan(
        FORWARD,
        0,
        (
            states,
            states_core,
            states_chip_out,
            states_chip,
            states_outer_out,
            states_outer,
            incoming_chip_out,
            incoming_chip,
            incoming_out,
            incoming,
        ),
    )
    back_scan = Scan(
        BACKWARD,
        1,
        (
            adjoints,
            adjoints_core,
            adjoints_chip_out,
            adjoints_chip,
            adjoints_outer_out,
            adjoints_outer,
            returned_chip_out,
            returned_chip,
            returned_out,
            returned,
        ),
    )

    for load in loads[3:6]:
        load.wait()

    def peer_piece(step):
        piece = (1 - core) * half + lax.rem((1 - chip) * outer + step, half)
        own_piece(piece)
        ahead_scan.core_copy(piece).start()

    loop(0, half, peer_piece)

    products = dot(read_ref[...], write_ref[...], NT)

    def within(piece, carry):
        at = columns(piece)
        inputs = x_ref[:, at]
        out = None
        for n in range(per_piece):
            head = piece * per_piece + n
            line = jnp.broadcast_to(cum_ref[pl.ds(head, 1), :], (rows, rows))
            decay = jnp.where(lower, jnp.exp(jnp.where(lower, line.T - line, 0.0)), 0.0)
            low = (decay * products).astype(BF16)
            decays[head] = decay
            weights[head] = low
            term = dot(low, inputs, NN)
            out = term if out is None else jnp.where(lane < n * mdim, out, term)
        mixer_out[:, at] = out
        return carry

    lax.fori_loop(0, size // 2, within, 0)

    def from_far(step):
        block = far_device(step, place)
        arrived(kbuf.at[block], KEY_OUTER, block, core_peer)
        arrived(vbuf.at[block], VALUE_OUTER, block, core_peer)
        start_keys(1, block, kbuf.at[block], vbuf.at[block], block, chip_peer)
        start_keys(2, block, kbuf.at[block], vbuf.at[block], block, core_peer)

    loop(1, outer, from_far)
    loop(0, half, lambda step: own_piece(core * half + step))
    chip_place = place + 2 - 4 * chip
    core_place = place + 1 - 2 * core

    lax.fori_loop(size // 2, size, within, 0)

    def from_chip(step):
        block = far_device(step, chip_place)
        arrived(kbuf.at[block], KEY_CHIP, block, core_peer)
        arrived(vbuf.at[block], VALUE_CHIP, block, core_peer)
        start_keys(2, block, kbuf.at[block], vbuf.at[block], block, core_peer)

    loop(0, outer, from_chip)

    def total_here(step):
        other = lax.rem(place + step, PLANE)
        arrived(totals.at[other], TOTAL, other, core_peer)

    loop(1, PLANE, total_here)
    ahead_scan.join()

    def from_core(step):
        for at in (core_place, 3 - place):
            block = far_device(step, at)
            arrived(kbuf.at[block], KEY_CORE, block, core_peer)
            arrived(vbuf.at[block], VALUE_CORE, block, core_peer)

    loop(0, outer, from_core)

    key_count = size * width
    query_count = heads * width
    key_index = lax.broadcasted_iota(jnp.int32, (key_count, query_count), 0)
    query_index = lax.broadcasted_iota(jnp.int32, (key_count, query_count), 1)
    key_place = lax.rem(key_index, width) * size + key_index // width
    query_place = lax.rem(query_index, width) * size + me
    visible = query_place >= key_place

    loads[6].wait()
    loads[7].wait()
    for block in range(blocks):
        span = slice(block * width, (block + 1) * width)
        own_queries = jnp.concatenate(
            [q_ref[span, h * head_dim : (h + 1) * head_dim] for h in range(heads)], axis=0
        )
        own_grads = jnp.concatenate(
            [do_ref[span, h * head_dim : (h + 1) * head_dim] for h in range(heads)], axis=0
        )
        highest = None
        for other in range(block + 1):
            span_k = slice(other * width, (other + 1) * width)
            key_block = kbuf[:, span_k, :].reshape(key_count, head_dim)
            scores = dot(key_block, own_queries, NT) * scale
            if other == block:
                scores = jnp.where(visible, scores, -1e30)
            exps[other] = scores
            top = jnp.max(scores, axis=0, keepdims=True)
            highest = top if highest is None else jnp.maximum(highest, top)
        total = jnp.zeros((1, query_count), F32)
        delta = jnp.zeros((1, query_count), F32)
        for other in range(block + 1):
            span_k = slice(other * width, (other + 1) * width)
            value_block = vbuf[:, span_k, :].reshape(key_count, head_dim)
            prob_grad = dot(value_block, own_grads, NT)
            raised = jnp.exp(exps[other] - highest)
            total = total + jnp.sum(raised, axis=0, keepdims=True)
            delta = delta + jnp.sum(raised * prob_grad, axis=0, keepdims=True)
            exps[other] = raised
            prob_grads[other] = prob_grad
        inverse = 1.0 / total
        delta = delta * inverse
        query_grad = jnp.zeros((query_count, head_dim), F32)
        for other in range(block + 1):
            span_k = slice(other * width, (other + 1) * width)
            key_block = kbuf[:, span_k, :].reshape(key_count, head_dim)
            probs = exps[other] * inverse
            score_grad = (probs * (prob_grads[other] - delta)).astype(BF16)
            query_grad = query_grad + dot(score_grad, key_block, TN)
            more_keys = (dot(score_grad, own_queries, NN) * scale).reshape(size, width, head_dim)
            more_values = dot(probs.astype(BF16), own_grads, NN).reshape(size, width, head_dim)
            if other == block:
                key_acc[other] = more_keys
                value_acc[other] = more_values
            else:
                key_acc[other] += more_keys
                value_acc[other] += more_values
        query_acc[block] = (query_grad * scale).reshape(heads, width, head_dim)
        pl.when(jnp.minimum(far, blocks - 1) == block)(ahead_scan.chain)

    per_block = width // per_partner
    for target in range(size):
        block, within_block = divmod(target, per_block)
        part = slice(within_block * per_partner, (within_block + 1) * per_partner)
        rows_out[target] = (
            query_acc[block, :, part, :].reshape(heads * per_partner, head_dim).astype(BF16)
        )
        target_far, target_place = divmod(target, PLANE)
        held = ((target_place % 2) * 2 + target_place // 2) * outer + target_far
        keys_out[held, :, :head_dim] = (
            key_acc[block, :, part, :].reshape(rows, head_dim).astype(BF16)
        )
        keys_out[held, :, head_dim:] = (
            value_acc[block, :, part, :].reshape(rows, head_dim).astype(BF16)
        )

    def grad_core_copy(which):
        span = pl.ds((2 * (1 - core) + which) * outer, outer)
        return copy_to(
            keys_out.at[span], keys_core.at[which], GRAD_CORE, which, which, core_peer
        )

    grad_core_copy(1 - chip).start()
    grad_core_copy(chip).start()

    def rows_copy(peer):
        return copy_to(rows_out.at[peer], rows_in.at[me], QUERY_ROWS, peer, me, peer)

    each_peer(lambda peer: rows_copy(peer).start())
    rows_in[me] = rows_out[me]
    ahead_scan.spread()

    def joined(which, j):
        return keys_out[(2 * core + which) * outer + j].astype(F32) + keys_core[
            which, j
        ].astype(F32)

    def grad_chip_copy():
        return copy_to(keys_chip_out, keys_chip, GRAD_CHIP, 0, 0, chip_peer)

    arrived(keys_core.at[1 - chip], GRAD_CORE, 1 - chip, core_peer)

    def far_grads(j):
        keys_chip_out[j] = joined(1 - chip, j).astype(BF16)

    loop(0, outer, far_grads)
    grad_chip_copy().start()
    arrived(keys_core.at[chip], GRAD_CORE, chip, core_peer)

    def carry_in(step, carry):
        piece = lax.rem(core * half + step, size)
        ahead_scan.result_here(piece)

        at = columns(piece)
        mixer_out[:, at] += grown[:, at] * dot(read_ref[...], incoming[piece], NT)
        return carry

    lax.fori_loop(0, size, carry_in, 0)

    def grad_outer_copy(other):
        return copy_to(
            keys_outer_out.at[other],
            keys_outer.at[far],
            GRAD_OUTER,
            other,
            far,
            other * PLANE + place,
        )

    arrived(keys_chip, GRAD_CHIP, 0, chip_peer)

    def outer_grads(step):
        other = lax.rem(far + step, outer)
        low = (joined(chip, other) + keys_chip[other].astype(F32)).astype(BF16)

        @pl.when(other == far)
        def _():
            keys_outer[far] = low

        @pl.when(other != far)
        def _():
            keys_outer_out[other] = low
            grad_outer_copy(other).start()

    loop(1, outer + 1, outer_grads)

    each_peer(lambda peer: arrived(rows_in.at[peer], QUERY_ROWS, peer, peer))

    def outer_here(step):
        other = lax.rem(far + step, outer)
        arrived(keys_outer.at[other], GRAD_OUTER, other, core_peer)

    loop(1, outer, outer_here)
    key_rows = keys_outer[0].astype(F32)
    for source in range(1, outer):
        key_rows = key_rows + keys_outer[source].astype(F32)
    shaped = rows_in[...].astype(F32).reshape(size, heads, per_partner, head_dim)
    grads = jnp.concatenate(
        [shaped[:, h].reshape(rows, head_dim).astype(BF16) for h in range(heads)]
        + [key_rows.astype(BF16)],
        axis=1,
    )
    token = lax.broadcasted_iota(jnp.int32, (rows, rows), 0)
    held_row = lax.broadcasted_iota(jnp.int32, (rows, rows), 1)
    order = (lax.rem(held_row, per_partner) * size + held_row // per_partner) == token
    grads = dot(jnp.where(order, 1.0, 0.0).astype(BF16), grads, NN).astype(BF16)
    loads[8].wait()
    loads[9].wait()
    loads[10].wait()

    def statistics(piece, carry):
        squares, crosses = carry
        at = columns(piece)
        down = pl.ds(pl.multiple_of(piece * LANES, LANES), LANES)
        rounded = dot(grads, weight[down, :], NT).astype(BF16).astype(F32)
        scaled = gain_ref[:, at] * rounded
        mixed[:, at] = scaled
        gate = gate_ref[:, at].astype(F32)
        gated = mixer_out[:, at] * (gate * jax.nn.sigmoid(gate))
        return (squares + gated * gated, crosses + scaled * gated)

    empty = jnp.zeros((rows, LANES), F32)
    squares, crosses = lax.fori_loop(0, size, statistics, (empty, empty))
    mean_square = jnp.sum(squares, axis=1, keepdims=True) / channels
    mean_cross = jnp.sum(crosses, axis=1, keepdims=True) / channels
    inverse_root = 1.0 / jnp.sqrt(mean_square + EPSILON)
    cross_factor = mean_cross * (inverse_root * inverse_root * inverse_root)

    def gate_piece(step, carry):
        piece = lax.rem((1 - core) * half + step, size)
        at = columns(piece)
        gate = gate_ref[:, at].astype(F32)
        sigmoid = jax.nn.sigmoid(gate)
        active = gate * sigmoid
        out = mixer_out[:, at]
        gated_grad = mixed[:, at] * inverse_root - out * active * cross_factor
        ggrad_ref[:, at] = gated_grad * out * sigmoid * (1.0 + gate * (1.0 - sigmoid))
        low = (gated_grad * active).astype(BF16)
        out_grad[:, at] = low
        raised = (low.astype(F32) * grown[:, at]).astype(BF16)
        grown_grad[:, at] = raised
        adjoints[piece] = dot(raised, read_ref[...], TN).astype(BF16)

        @pl.when(piece // half != core)
        def _():
            back_scan.core_copy(piece).start()

        return carry

    lax.fori_loop(0, size, gate_piece, 0)
    back_scan.join()

    def grads_within(piece, read_grad):
        at = columns(piece)
        grad_piece = out_grad[:, at]
        inputs = x_ref[:, at]
        out = None
        pairs = jnp.zeros((rows, rows), F32)
        for n in range(per_piece):
            head = piece * per_piece + n
            term = dot(weights[head], grad_piece, TN)
            out = term if out is None else jnp.where(lane < n * mdim, out, term)
            here = (lane >= n * mdim) & (lane < (n + 1) * mdim)
            alone = jnp.where(here, grad_piece.astype(F32), 0.0).astype(BF16)
            pairs = pairs + decays[head] * dot(alone, inputs, NT)
        igrad_ref[:, at] = out
        pair_sum[...] += pairs
        return read_grad + dot(grown_grad[:, at], incoming[piece], NN)

    pair_sum[...] = jnp.zeros((rows, rows), F32)
    read_grad = jnp.zeros((rows, nstate), F32)
    per_part = size // blocks
    for part in range(blocks):
        read_grad = lax.fori_loop(
            part * per_part, (part + 1) * per_part, grads_within, read_grad
        )
        pl.when(jnp.minimum(outer - 1 - far, blocks - 1) == part)(back_scan.chain)
    back_scan.spread()
    pairs_low = pair_sum[...].astype(BF16)
    rgrad_ref[...] = read_grad + dot(pairs_low, write_ref[...], NN)

    def finish(step, write_grad):
        piece = lax.rem(core * half + step, size)
        back_scan.result_here(piece)

        at = columns(piece)
        igrad_ref[:, at] += remain[:, at] * dot(write_ref[...], returned[piece], NT)
        return write_grad + dot(remain_input[:, at], returned[piece], NN)

    wgrad_ref[...] = lax.fori_loop(0, size, finish, dot(pairs_low, read_ref[...], TN))

    def wait_keys(*arguments):
        for each in key_copies(*arguments):
            each.wait_send()

    def keys_sent(step):
        peer = far_device(step, place)
        wait_keys(0, me, kbuf.at[me], vbuf.at[me], peer, peer)

    def keys_relayed(step):
        block = far_device(step, place)
        wait_keys(1, block, kbuf.at[block], vbuf.at[block], block, chip_peer)
        wait_keys(2, block, kbuf.at[block], vbuf.at[block], block, core_peer)
        block = far_device(step, chip_place)
        wait_keys(2, block, kbuf.at[block], vbuf.at[block], block, core_peer)

    loop(1, outer, keys_sent)
    loop(0, outer, keys_relayed)
    loop(1, PLANE, lambda step: total_copy(step).wait_send())
    each_peer(lambda peer: rows_copy(peer).wait_send())
    grad_core_copy(0).wait_send()
    grad_core_copy(1).wait_send()
    grad_chip_copy().wait_send()
    loop(1, outer, lambda step: grad_outer_copy(lax.rem(far + step, outer)).wait_send())
    ahead_scan.sent()
    back_scan.sent()


def hand_over(*refs):
    done = refs[-1]
    copies = [
        pltpu.make_async_copy(refs[n], refs[n + 4], done.at[n]) for n in range(4)
    ]
    for copy in copies:
        copy.start()
    for copy in copies:
        copy.wait()


def fused_body(
    queries,
    keys,
    values,
    d_out,
    mixer_input,
    gate_input,
    state_write,
    state_read,
    log_decay,
    norm_gain,
    project_weight,
):
    arguments = (
        queries,
        keys,
        values,
        d_out,
        mixer_input,
        gate_input,
        state_write,
        state_read,
        log_decay,
        norm_gain,
        project_weight,
    )
    size = lax.axis_size("ctx")
    rows, head_dim = keys.shape
    heads = queries.shape[1] // head_dim
    channels = mixer_input.shape[1]
    mheads = log_decay.shape[1]
    mdim = channels // mheads
    nstate = state_write.shape[1]
    blocks = 4
    width = rows // blocks
    per_partner = rows // size
    if channels != size * LANES or LANES % mdim or per_partner % 8 or width % per_partner or size % PLANE or size % blocks:
        return body(*arguments)
    per_piece = LANES // mdim
    key_count = size * width
    query_count = heads * width
    outer = size // PLANE
    pieces = pltpu.VMEM((size, LANES, nstate), BF16)
    fewer = pltpu.VMEM((outer, LANES, nstate), BF16)
    scan_buffers = [pieces] * 4 + [fewer] * 2 + [pieces] * 4
    scratch = [
        pltpu.VMEM(queries.shape, BF16),
        pltpu.VMEM(d_out.shape, BF16),
        pltpu.VMEM(mixer_input.shape, BF16),
        pltpu.VMEM(gate_input.shape, BF16),
        pltpu.VMEM(state_write.shape, BF16),
        pltpu.VMEM(state_read.shape, BF16),
        pltpu.VMEM((mheads, rows), F32),
        pltpu.VMEM((1, channels), F32),
        pltpu.VMEM((mheads, rows), F32),
        pltpu.VMEM((size, rows, head_dim), BF16),
        pltpu.VMEM((size, rows, head_dim), BF16),
        pltpu.VMEM((mheads, LANES), F32),
        pltpu.VMEM((PLANE, mheads, LANES), F32),
        pltpu.VMEM((size, heads * per_partner, head_dim), BF16),
        pltpu.VMEM((size, heads * per_partner, head_dim), BF16),
        pltpu.VMEM((size, rows, 2 * head_dim), BF16),
        pltpu.VMEM((2, outer, rows, 2 * head_dim), BF16),
        pltpu.VMEM((outer, rows, 2 * head_dim), BF16),
        pltpu.VMEM((outer, rows, 2 * head_dim), BF16),
        pltpu.VMEM((outer, rows, 2 * head_dim), BF16),
        pltpu.VMEM((outer, rows, 2 * head_dim), BF16),
        *scan_buffers,
        *scan_buffers,
        pltpu.VMEM((blocks, key_count, query_count), F32),
        pltpu.VMEM((blocks, key_count, query_count), F32),
        pltpu.VMEM((blocks, size, width, head_dim), F32),
        pltpu.VMEM((blocks, size, width, head_dim), F32),
        pltpu.VMEM((blocks, heads, width, head_dim), F32),
        pltpu.VMEM((mheads, rows, rows), F32),
        pltpu.VMEM((mheads, rows, rows), BF16),
        pltpu.VMEM((rows, channels), F32),
        pltpu.VMEM((rows, channels), F32),
        pltpu.VMEM((rows, channels), F32),
        pltpu.VMEM((rows, channels), F32),
        pltpu.VMEM((rows, channels), BF16),
        pltpu.VMEM((rows, channels), BF16),
        pltpu.VMEM((rows, channels), BF16),
        pltpu.VMEM((rows, rows), F32),
        pltpu.VMEM(project_weight.shape, project_weight.dtype),
        pltpu.SemaphoreType.DMA((11,)),
        pltpu.SemaphoreType.DMA((PHASES, size)),
        pltpu.SemaphoreType.DMA((PHASES, size)),
    ]
    vmem = pl.BlockSpec(memory_space=pltpu.VMEM)
    results = pl.pallas_call(
        functools.partial(fused_kernel, size, mdim),
        out_shape=(
            pltpu.VMEM((rows, channels), F32),
            pltpu.VMEM((rows, channels), F32),
            pltpu.VMEM((rows, nstate), F32),
            pltpu.VMEM((rows, nstate), F32),
        ),
        in_specs=[pl.BlockSpec(memory_space=pl.ANY)] * 11,
        out_specs=(vmem,) * 4,
        scratch_shapes=scratch,
        compiler_params=pltpu.CompilerParams(
            collective_id=0, has_side_effects=True, vmem_limit_bytes=56 * 1024 * 1024
        ),
    )(
        queries,
        keys,
        values,
        d_out,
        mixer_input,
        gate_input,
        state_write,
        state_read,
        log_decay.T,
        norm_gain[None, :],
        project_weight,
    )
    anywhere = pl.BlockSpec(memory_space=pl.ANY)
    return pl.pallas_call(
        hand_over,
        out_shape=tuple(jax.ShapeDtypeStruct(r.shape, r.dtype) for r in results),
        in_specs=[anywhere] * 4,
        out_specs=(anywhere,) * 4,
        scratch_shapes=[pltpu.SemaphoreType.DMA((4,))],
    )(*[pltpu.with_memory_space_constraint(r, pltpu.VMEM) for r in results])


def solution(mesh):
    placed = (
        P("ctx", "groups"),
        P("ctx", "groups"),
        P("ctx", "groups"),
        P("ctx", "groups"),
        P("ctx", "groups"),
        P("ctx", "groups"),
        P("ctx", "groups"),
        P("ctx", "groups"),
        P("ctx", "groups"),
        P("groups"),
        P(None, "groups"),
    )
    return jax.shard_map(
        fused_body,
        mesh=mesh,
        in_specs=placed,
        out_specs=(P("ctx", "groups"), P("ctx", "groups"), P("ctx", "groups"), P("ctx", "groups")),
        check_vma=False,
    )
```

```python
import functools
import math

import jax
import jax.numpy as jnp
from jax import lax
from jax.experimental import pallas as pl
from jax.experimental.pallas import tpu as pltpu
from jax.sharding import PartitionSpec as P

EPSILON = 1e-05
HIGHEST = lax.Precision.HIGHEST


def carried_in(part, axis, combine, identity, reverse):
    count = lax.axis_size(axis)
    place = lax.axis_index(axis)
    ahead = count - 1 - place if reverse else place
    gathered = jax.tree.map(lambda a: lax.all_gather(a, axis), part)
    state = jax.tree.map(lambda a, e: jnp.zeros_like(a) + jnp.asarray(e, a.dtype), part, identity)

    def one(hop, state):
        source = count - 1 - hop if reverse else hop
        return combine(
            state, jax.tree.map(lambda a: lax.dynamic_index_in_dim(a, source, 0, False), gathered)
        )

    return lax.fori_loop(0, ahead, one, state)


def decay_parts(log_decay):
    length = log_decay.shape[0]
    lower = jnp.tril(jnp.ones((length, length), jnp.float32))
    cumulated = jnp.dot(lower, log_decay, precision=HIGHEST)
    causal_mask = (jnp.arange(length)[:, None] >= jnp.arange(length)[None, :])[None, :, :]
    spread = cumulated.T[:, :, None] - cumulated.T[:, None, :]
    decays = jnp.where(causal_mask, jnp.exp(jnp.where(causal_mask, spread, 0.0)), 0.0)
    remaining = jnp.exp(cumulated[-1][None, :] - cumulated)
    return (cumulated, decays, remaining)


def local_state(values_f, write_f, remaining):
    return jnp.einsum("shp,sn->hpn", values_f * remaining[:, :, None], write_f, precision=HIGHEST)


def block_output(weights, values_f, read_f, cumulated, incoming):
    within = jnp.einsum("hts,shp->thp", weights, values_f, precision=HIGHEST)
    carried = jnp.einsum("hpn,tn->thp", incoming, read_f, precision=HIGHEST)
    return within + jnp.exp(cumulated)[:, :, None] * carried


def local_adjoint(grads_f, read_f, cumulated):
    return jnp.einsum(
        "thp,tn->hpn", grads_f * jnp.exp(cumulated)[:, :, None], read_f, precision=HIGHEST
    )


def block_grads(
    weights, decays, values_f, grads_f, write_f, read_f, cumulated, remaining, incoming, adjoint
):
    value_grad = jnp.einsum("hts,thp->shp", weights, grads_f, precision=HIGHEST)
    value_grad = value_grad + remaining[:, :, None] * jnp.einsum(
        "hpn,sn->shp", adjoint, write_f, precision=HIGHEST
    )
    pairs = jnp.einsum("thp,shp->hts", grads_f, values_f, precision=HIGHEST)
    pair_sum = jnp.sum(decays * pairs, axis=0)
    read_grad = jnp.dot(pair_sum, write_f, precision=HIGHEST) + jnp.einsum(
        "thp,hpn->tn", grads_f * jnp.exp(cumulated)[:, :, None], incoming, precision=HIGHEST
    )
    write_grad = jnp.dot(pair_sum.T, read_f, precision=HIGHEST) + jnp.einsum(
        "shp,hpn->sn", values_f * remaining[:, :, None], adjoint, precision=HIGHEST
    )
    return (value_grad, write_grad, read_grad)


def gate_grads(mixer_out, gate_input, norm_gain, mixer_grad):
    gate_f = gate_input.astype(jnp.float32)
    sigmoid = jax.nn.sigmoid(gate_f)
    active = gate_f * sigmoid
    gated = mixer_out * active
    root_mean = jnp.sqrt(jnp.mean(gated * gated, axis=-1, keepdims=True) + EPSILON)
    scaled = norm_gain[None, :] * mixer_grad.astype(jnp.float32)
    gated_grad = (
        scaled / root_mean - gated * jnp.mean(scaled * gated, axis=-1, keepdims=True) / root_mean**3
    )
    gate_gradient = gated_grad * mixer_out * sigmoid * (1.0 + gate_f * (1.0 - sigmoid))
    out_grad = (gated_grad * active).astype(jnp.bfloat16)
    return (out_grad, gate_gradient)


def compose(earlier, later):
    return (earlier[0] * later[0], later[0][:, None, None] * earlier[1] + later[1])


def token_order(received, ctx_size, rows):
    per_partner = rows // ctx_size
    return received.reshape(ctx_size, per_partner, -1).transpose(1, 0, 2).reshape(rows, -1)


def apply_weight(grad_rows, project_weight):
    return lax.dot_general(
        grad_rows, project_weight, (((1,), (1,)), ((), ())), preferred_element_type=jnp.float32
    ).astype(jnp.bfloat16)


def body(
    queries,
    keys,
    values,
    d_out,
    mixer_input,
    gate_input,
    state_write,
    state_read,
    log_decay,
    norm_gain,
    project_weight,
):
    ctx_size = lax.axis_size("ctx")
    ctx_index = lax.axis_index("ctx")
    rows = keys.shape[0]
    head_dim = keys.shape[1]
    heads = queries.shape[1] // head_dim
    scale = 1.0 / math.sqrt(head_dim)
    query_heads = queries.reshape(rows, heads, head_dim)
    grad_heads = d_out.reshape(rows, heads, head_dim)
    query_pos = jnp.arange(rows, dtype=jnp.int32) * ctx_size + ctx_index
    mheads = log_decay.shape[1]
    channels = mixer_input.shape[1]
    mdim = channels // mheads
    values_f = mixer_input.astype(jnp.float32).reshape(rows, mheads, mdim)
    write_f = state_write.astype(jnp.float32)
    read_f = state_read.astype(jnp.float32)
    cumulated, decays, remaining = decay_parts(log_decay)
    products = jnp.dot(state_read, state_write.T, preferred_element_type=jnp.float32)
    weights = decays * products[None, :, :]
    own_state = local_state(values_f, write_f, remaining)
    passing = jnp.exp(cumulated[-1])
    identity = (jnp.ones_like(passing), jnp.zeros_like(own_state))
    _, incoming = carried_in((passing, own_state), "ctx", compose, identity, False)
    all_keys, all_values = (
        lax.all_gather(keys, "ctx", axis=0, tiled=True),
        lax.all_gather(values, "ctx", axis=0, tiled=True),
    )
    total = all_keys.shape[0]
    total_rows = jnp.arange(total, dtype=jnp.int32)
    key_pos = total_rows % rows * ctx_size + total_rows // rows
    width = math.gcd(total, 512)
    count = total // width
    key_blocks = all_keys.reshape(count, width, head_dim)
    value_blocks = all_values.reshape(count, width, head_dim)
    place_blocks = key_pos.reshape(count, width)

    def scores_of(key_block, place_block):
        raw_scores = (
            jnp.einsum("qhe,ke->qhk", query_heads, key_block, preferred_element_type=jnp.float32)
            * scale
        )
        visible = query_pos[:, None, None] >= place_block[None, None, :]
        return jnp.where(visible, raw_scores, -jnp.inf)

    def total_step(carry, block):
        running_max, running_sum = carry
        masked = scores_of(block[0], block[1])
        new_max = jnp.maximum(running_max, jnp.max(masked, axis=-1))
        running_sum = running_sum * jnp.exp(running_max - new_max) + jnp.sum(
            jnp.exp(masked - new_max[:, :, None]), axis=-1
        )
        return ((new_max, running_sum), None)

    start_max = jnp.full((rows, heads), -1e30, jnp.float32)
    start_sum = jnp.zeros((rows, heads), jnp.float32)
    (final_max, final_sum), _ = lax.scan(
        total_step, (start_max, start_sum), (key_blocks, place_blocks)
    )
    log_total = final_max + jnp.log(final_sum)

    def output_step(carry, block):
        masked = scores_of(block[0], block[1])
        probs_low = jnp.exp(masked - log_total[:, :, None]).astype(jnp.bfloat16)
        return (
            carry
            + jnp.einsum("qhk,kd->qhd", probs_low, block[2], preferred_element_type=jnp.float32),
            None,
        )

    attention_out, _ = lax.scan(
        output_step,
        jnp.zeros((rows, heads, head_dim), jnp.float32),
        (key_blocks, place_blocks, value_blocks),
    )
    delta = jnp.sum(grad_heads.astype(jnp.float32) * attention_out, axis=-1)

    def score_parts(block):
        masked = scores_of(block[0], block[1])
        probs_f = jnp.exp(masked - log_total[:, :, None])
        prob_grad = jnp.einsum(
            "qhd,kd->qhk", grad_heads, block[2], preferred_element_type=jnp.float32
        )
        score_grad = (probs_f * (prob_grad - delta[:, :, None])).astype(jnp.bfloat16)
        return (probs_f.astype(jnp.bfloat16), score_grad)

    start_query = jnp.zeros((rows, heads, head_dim), jnp.float32)

    def query_step(carry, block):
        probs_low, score_grad = score_parts(block)
        return (
            carry
            + jnp.einsum("qhk,ke->qhe", score_grad, block[0], preferred_element_type=jnp.float32),
            None,
        )

    query_acc, _ = lax.scan(query_step, start_query, (key_blocks, place_blocks, value_blocks))
    all_queries, all_grads = (
        lax.all_gather(queries, "ctx", axis=0, tiled=True),
        lax.all_gather(d_out, "ctx", axis=0, tiled=True),
    )
    all_totals, all_deltas = (
        lax.all_gather(log_total, "ctx", axis=0, tiled=True),
        lax.all_gather(delta, "ctx", axis=0, tiled=True),
    )
    query_blocks = all_queries.reshape(count, width, heads, head_dim)
    grad_blocks = all_grads.reshape(count, width, heads, head_dim)
    total_blocks = all_totals.reshape(count, width, heads)
    delta_blocks = all_deltas.reshape(count, width, heads)

    def key_step(carry, block):
        key_acc, value_acc = carry
        query_block, grad_block, total_block, delta_block, place_block = block
        raw_scores = (
            jnp.einsum("qhe,ke->qhk", query_block, keys, preferred_element_type=jnp.float32) * scale
        )
        visible = place_block[:, None, None] >= query_pos[None, None, :]
        masked = jnp.where(visible, raw_scores, -jnp.inf)
        probs_f = jnp.exp(masked - total_block[:, :, None])
        probs_low = probs_f.astype(jnp.bfloat16)
        prob_grad = jnp.einsum(
            "qhd,kd->qhk", grad_block, values, preferred_element_type=jnp.float32
        )
        score_grad = (probs_f * (prob_grad - delta_block[:, :, None])).astype(jnp.bfloat16)
        key_acc = (
            key_acc
            + jnp.einsum("qhk,qhe->ke", score_grad, query_block, preferred_element_type=jnp.float32)
            * scale
        )
        value_acc = value_acc + jnp.einsum(
            "qhk,qhd->kd", probs_low, grad_block, preferred_element_type=jnp.float32
        )
        return ((key_acc, value_acc), None)

    empty_keys = jnp.zeros((rows, head_dim), jnp.float32)
    (key_acc, value_acc), _ = lax.scan(
        key_step,
        (empty_keys, empty_keys),
        (query_blocks, grad_blocks, total_blocks, delta_blocks, place_blocks),
    )
    key_grad = key_acc.astype(jnp.bfloat16)
    value_grad = value_acc.astype(jnp.bfloat16)
    query_grad = (query_acc * scale).astype(jnp.bfloat16).reshape(rows, heads * head_dim)
    projected = jnp.concatenate([query_grad, key_grad, value_grad], axis=1)
    mixed = apply_weight(projected, project_weight)
    mixer_grad = token_order(
        lax.all_to_all(mixed, "ctx", split_axis=0, concat_axis=0, tiled=True), ctx_size, rows
    )
    mixer_out = block_output(weights, values_f, read_f, cumulated, incoming).reshape(rows, channels)
    out_grad, gate_gradient = gate_grads(mixer_out, gate_input, norm_gain, mixer_grad)
    grads_f = out_grad.astype(jnp.float32).reshape(rows, mheads, mdim)
    own_adjoint = local_adjoint(grads_f, read_f, cumulated)
    _, adjoint = carried_in((passing, own_adjoint), "ctx", compose, identity, True)
    input_grad, write_gradient, read_gradient = block_grads(
        weights, decays, values_f, grads_f, write_f, read_f, cumulated, remaining, incoming, adjoint
    )
    return (input_grad.reshape(rows, channels), gate_gradient, write_gradient, read_gradient)


F32 = jnp.float32
BF16 = jnp.bfloat16
MESH = pl.DeviceIdType.MESH
LANES = 128
(
    KEY_OUTER,
    KEY_CHIP,
    KEY_CORE,
    VALUE_OUTER,
    VALUE_CHIP,
    VALUE_CORE,
    TOTAL,
    QUERY_ROWS,
    GRAD_CORE,
    GRAD_CHIP,
    GRAD_OUTER,
) = range(11)
FORWARD = 11
BACKWARD = 16
PHASES = 21
PLANE = 4
LOG2E = 1.0 / math.log(2.0)


def dot(a, b, dims):
    return lax.dot_general(a, b, (dims, ((), ())), preferred_element_type=F32)


NN = ((1,), (0,))
NT = ((1,), (1,))
TN = ((0,), (0,))


def split(array, terms):
    parts = []
    for _ in range(terms):
        low = array.astype(BF16)
        parts.append(low)
        array = array - low.astype(F32)
    return parts


def fused_kernel(
    size,
    mdim,
    q_hbm,
    k_hbm,
    v_hbm,
    do_hbm,
    x_hbm,
    gate_hbm,
    write_hbm,
    read_hbm,
    decay_hbm,
    gain_hbm,
    weight_hbm,
    igrad_ref,
    ggrad_ref,
    wgrad_ref,
    rgrad_ref,
    q_ref,
    do_ref,
    x_ref,
    gate_ref,
    write_ref,
    read_ref,
    decay_ref,
    gain_ref,
    cum_ref,
    write_turned,
    read_turned,
    kbuf,
    vbuf,
    own_totals,
    totals,
    rows_out,
    rows_in,
    keys_out,
    keys_core,
    keys_chip_out,
    keys_chip,
    keys_outer_out,
    keys_outer,
    states,
    states_core,
    states_chip_out,
    states_chip,
    states_outer_out,
    states_outer,
    incoming_chip_out,
    incoming_chip,
    incoming_out,
    incoming,
    adjoints,
    adjoints_core,
    adjoints_chip_out,
    adjoints_chip,
    adjoints_outer_out,
    adjoints_outer,
    returned_chip_out,
    returned_chip,
    returned_out,
    returned,
    exps,
    prob_grads,
    key_acc,
    value_acc,
    decays,
    weights,
    grown,
    remain,
    mixer_out,
    mixed,
    out_grad,
    grown_grad,
    remain_input,
    pair_sum,
    weight,
    load_sem,
    ssem,
    rsem,
):
    me = lax.axis_index("ctx")
    _, rows, head_dim = kbuf.shape
    heads = q_ref.shape[1] // head_dim
    channels = x_ref.shape[1]
    mheads = cum_ref.shape[0]
    per_piece = LANES // mdim
    blocks = key_acc.shape[0]
    width = rows // blocks
    per_partner = rows // size
    scale = 1.0 / math.sqrt(head_dim)

    outer = size // PLANE
    place = lax.rem(me, PLANE)
    core = lax.rem(me, 2)
    chip = place // 2
    far = me // PLANE
    core_peer = me + 1 - 2 * core
    chip_peer = me + 2 - 4 * chip
    nstate = write_ref.shape[1]
    span = PLANE * LANES

    def copy_to(src, dst, phase, sent_at, landed_at, peer):
        return pltpu.make_async_remote_copy(
            src_ref=src,
            dst_ref=dst,
            send_sem=ssem.at[phase, sent_at],
            recv_sem=rsem.at[phase, landed_at],
            device_id={"ctx": peer},
            device_id_type=MESH,
        )

    def arrived(dst, phase, at, peer):
        copy_to(dst, dst, phase, at, at, peer).wait_recv()

    def loop(first, last, fn):
        def one(step, carry):
            fn(step)
            return carry

        lax.fori_loop(first, last, one, 0)

    def each_peer(fn):
        loop(1, size, lambda step: fn(lax.rem(me + step, size)))

    def columns(piece):
        return pl.ds(pl.multiple_of(piece * LANES, LANES), LANES)

    def chunk_columns(j):
        return pl.ds(pl.multiple_of(j * span, span), span)

    loads = [
        pltpu.make_async_copy(source, target, load_sem.at[n])
        for n, (source, target) in enumerate(
            (
                (k_hbm, kbuf.at[me]),
                (v_hbm, vbuf.at[me]),
                (decay_hbm, decay_ref),
                (x_hbm, x_ref),
                (write_hbm, write_ref),
                (read_hbm, read_ref),
                (q_hbm, q_ref),
                (do_hbm, do_ref),
                (gain_hbm, gain_ref),
                (gate_hbm, gate_ref),
                (weight_hbm, weight),
            )
        )
    ]
    for load in loads:
        load.start()
    barrier = pltpu.get_barrier_semaphore()

    def greet(peer):
        pl.semaphore_signal(barrier, inc=1, device_id={"ctx": peer}, device_id_type=MESH)

    each_peer(greet)
    loads[2].wait()
    upper = (
        lax.broadcasted_iota(jnp.int32, (rows, rows), 0)
        <= lax.broadcasted_iota(jnp.int32, (rows, rows), 1)
    ).astype(F32)
    cumulated = lax.dot_general(
        decay_ref[...], upper, (NN, ((), ())), precision=HIGHEST, preferred_element_type=F32
    )
    cum_ref[...] = cumulated * LOG2E
    own = jnp.exp(cumulated)
    left = jnp.exp(cumulated[:, rows - 1 : rows] - cumulated)
    chosen_head = lax.broadcasted_iota(jnp.int32, (2 * mheads, channels), 1) // mdim
    chooses = lax.rem(lax.broadcasted_iota(jnp.int32, (2 * mheads, channels), 0), mheads)
    chosen = jnp.where(chosen_head == chooses, 1.0, 0.0).astype(BF16)
    grown[...] = dot(jnp.concatenate(split(own.T, 2), axis=1), chosen, NN)
    remain[...] = dot(jnp.concatenate(split(left.T, 2), axis=1), chosen, NN)
    all_totals = grown[rows - 1 : rows, :]
    own_totals[...] = all_totals
    totals[place] = all_totals
    for load in loads[3:6]:
        load.wait()
    write_turned[...] = write_ref[...].T
    read_turned[...] = read_ref[...].T
    loads[0].wait()
    loads[1].wait()
    pl.semaphore_wait(barrier, size - 1)

    keys_kind = (KEY_OUTER, kbuf)
    values_kind = (VALUE_OUTER, vbuf)

    def relay(kind, hop, block, peer, sent_at):
        base, held = kind
        return copy_to(held.at[block], held.at[block], base + hop, sent_at, block, peer)

    def landed(kind, hop, block):
        base, held = kind
        arrived(held.at[block], base + hop, block, core_peer)

    def far_device(step, at):
        return lax.rem(far + step, outer) * PLANE + at

    def at_distance(distance, fn):
        pl.when(far - distance >= 0)(lambda: fn(far - distance))
        pl.when(far + distance < outer)(lambda: fn(far + distance))

    def outer_relay(kind, plane):
        peer = plane * PLANE + place
        return relay(kind, 0, me, peer, peer)

    def chip_relay(kind, block):
        return relay(kind, 1, block, chip_peer, block)

    def core_relay(kind, block):
        return relay(kind, 2, block, core_peer, block)

    def total_copy(step):
        other = lax.rem(place + step, PLANE)
        return copy_to(
            own_totals, totals.at[place], TOTAL, other, place, far * PLANE + other
        )

    loop(1, PLANE, lambda step: total_copy(step).start())
    for kind in (keys_kind, values_kind):
        for distance in range(1, outer):
            at_distance(distance, lambda plane: outer_relay(kind, plane).start())
        chip_relay(kind, me).start()
        core_relay(kind, me).start()

    lane = lax.broadcasted_iota(jnp.int32, (rows, LANES), 1)
    row = lax.broadcasted_iota(jnp.int32, (rows, LANES), 0)
    lower = row >= lane
    wide_row = lax.broadcasted_iota(jnp.int32, (rows, per_piece * rows), 0)
    wide_lane = lax.broadcasted_iota(jnp.int32, (rows, per_piece * rows), 1)
    wide_lower = wide_row >= lax.rem(wide_lane, rows)
    row_lane = lax.broadcasted_iota(jnp.int32, (1, LANES), 1)
    head_masks = [
        jnp.where(row_lane // mdim == n, 1.0, 0.0).astype(BF16) for n in range(per_piece)
    ]

    class Scan:
        def __init__(self, base, lead, buffers):
            self.base, self.lead = base, lead
            (
                self.own,
                self.core,
                self.chip_out,
                self.chip,
                self.outer_out,
                self.outer,
                self.back_chip_out,
                self.back_chip,
                self.back_out,
                self.result,
            ) = buffers

        def factor(self, source, piece):
            return totals[source, :, columns(piece)]

        def chip_factor(self, which, piece):
            return self.factor(2 * which, piece) * self.factor(2 * which + 1, piece)

        def core_copy(self, piece):
            return copy_to(
                self.own.at[piece], self.core.at[piece], self.base, piece, piece, core_peer
            )

        def chip_copy(self, piece):
            return copy_to(
                self.chip_out.at[piece],
                self.chip.at[piece],
                self.base + 1,
                piece,
                piece,
                chip_peer,
            )

        def outer_copy(self, j):
            ahead = me - PLANE if self.lead else me + PLANE
            ahead = lax.rem(ahead + size, size)
            return copy_to(
                self.outer_out.at[j], self.outer.at[j], self.base + 2, j, j, ahead
            )

        def back_chip_copy(self, piece):
            return copy_to(
                self.back_chip_out.at[piece],
                self.back_chip.at[piece],
                self.base + 3,
                piece,
                piece,
                chip_peer,
            )

        def back_copy(self, piece):
            return copy_to(
                self.back_out.at[piece],
                self.result.at[piece],
                self.base + 4,
                piece,
                piece,
                core_peer,
            )

        def owned(self, which_core, which_chip, j):
            return j * PLANE + 2 * which_core + which_chip

        def quarter(self, which, j):
            return self.owned(core, which, j)

        def core_states(self, piece):
            own = self.own[piece].astype(F32)
            other = self.core[piece].astype(F32)
            leads = core == self.lead
            return jnp.where(leads, own, other), jnp.where(leads, other, own)

        def core_source(self, which):
            return 2 * chip + which

        def send_core(self, j):
            for which in range(2):
                self.core_copy(self.owned(1 - core, which, j)).start()

        def join_cores(self, piece):
            arrived(self.core.at[piece], self.base, piece, core_peer)
            first, second = self.core_states(piece)
            later = self.factor(self.core_source(1 - self.lead), piece)
            self.chip_out[piece] = (later * first + second).astype(BF16)

        def join(self, j):
            piece = self.quarter(1 - chip, j)
            self.join_cores(piece)
            self.chip_copy(piece).start()
            self.join_cores(self.quarter(chip, j))

        def chain_parts(self, j):
            leads = chip == self.lead
            piece = self.quarter(chip, j)
            own = self.chip_out[piece].astype(F32)
            other = self.chip[piece].astype(F32)
            first = jnp.where(leads, own, other)
            second = jnp.where(leads, other, own)
            state = self.outer[j].astype(F32)
            middle = self.chip_factor(self.lead, piece) * state + first
            return piece, leads, state, middle, second

        def chain_on(self, j):
            opens = far == (outer - 1 if self.lead else 0)
            closes = far == (0 if self.lead else outer - 1)
            piece = self.quarter(chip, j)
            arrived(self.chip.at[piece], self.base + 1, piece, chip_peer)

            @pl.when(opens)
            def _():
                self.outer[j] = jnp.zeros((nstate, LANES), BF16)

            @pl.when(jnp.logical_not(opens))
            def _():
                arrived(self.outer.at[j], self.base + 2, j, core_peer)

            @pl.when(jnp.logical_not(closes))
            def _():
                piece, leads, state, middle, second = self.chain_parts(j)
                late = self.chip_factor(1 - self.lead, piece)
                self.outer_out[j] = (late * middle + second).astype(BF16)
                self.outer_copy(j).start()

        def chain_back(self, j):
            piece, leads, state, middle, _ = self.chain_parts(j)
            self.back_chip_out[piece] = jnp.where(leads, middle, state).astype(BF16)
            self.back_chip_copy(piece).start()
            self.back_chip[piece] = jnp.where(leads, state, middle).astype(BF16)

        def hand_back(self, piece):
            state = self.back_chip[piece].astype(F32)
            first, _ = self.core_states(piece)
            middle = self.factor(self.core_source(self.lead), piece) * state + first
            leads = core == self.lead
            self.back_out[piece] = jnp.where(leads, middle, state).astype(BF16)
            self.back_copy(piece).start()
            self.result[piece] = jnp.where(leads, state, middle).astype(BF16)

        def hand_back_near(self, j):
            self.hand_back(self.quarter(chip, j))

        def hand_back_far(self, j):
            piece = self.quarter(1 - chip, j)
            arrived(self.back_chip.at[piece], self.base + 3, piece, chip_peer)
            self.hand_back(piece)

        def results_here(self, j):
            for which in range(2):
                piece = self.owned(1 - core, which, j)
                arrived(self.result.at[piece], self.base + 4, piece, core_peer)

        def results(self, j):
            return jnp.concatenate(
                [self.result[j * PLANE + n] for n in range(PLANE)], axis=1
            )

        def store_own(self, j, wide):
            for n in range(PLANE):
                self.own[j * PLANE + n] = wide[:, n * LANES : (n + 1) * LANES].astype(BF16)

        def sent(self):
            closes = far == (0 if self.lead else outer - 1)

            def one(j):
                for which in range(2):
                    self.core_copy(self.owned(1 - core, which, j)).wait_send()
                    self.back_copy(self.owned(core, which, j)).wait_send()
                self.chip_copy(self.quarter(1 - chip, j)).wait_send()
                self.back_chip_copy(self.quarter(chip, j)).wait_send()

                @pl.when(jnp.logical_not(closes))
                def _():
                    self.outer_copy(j).wait_send()

            loop(0, outer, one)

    ahead_scan = Scan(
        FORWARD,
        0,
        (
            states,
            states_core,
            states_chip_out,
            states_chip,
            states_outer_out,
            states_outer,
            incoming_chip_out,
            incoming_chip,
            incoming_out,
            incoming,
        ),
    )
    back_scan = Scan(
        BACKWARD,
        1,
        (
            adjoints,
            adjoints_core,
            adjoints_chip_out,
            adjoints_chip,
            adjoints_outer_out,
            adjoints_outer,
            returned_chip_out,
            returned_chip,
            returned_out,
            returned,
        ),
    )

    def forward_chain(plane, first, end):
        def one(j):
            ahead_scan.chain_on(j)
            ahead_scan.chain_back(j)

        pl.when(far == plane)(lambda: loop(first, end, one))

    def own_chunk(j):
        at = chunk_columns(j)
        scaled_input = (x_ref[:, at].astype(F32) * remain[:, at]).astype(BF16)
        remain_input[:, at] = scaled_input
        ahead_scan.store_own(j, dot(write_turned[...], scaled_input, NN))
        ahead_scan.send_core(j)

    turned = jnp.concatenate(split(cum_ref[...].T, 3), axis=1)
    products = dot(read_ref[...], write_ref[...], NT)
    wide_products = jnp.concatenate([products] * per_piece, axis=1)
    turned_head = lax.rem(
        lax.broadcasted_iota(jnp.int32, (3 * mheads, per_piece * rows), 0), mheads
    )
    head_of_lane = (
        lax.broadcasted_iota(jnp.int32, (3 * mheads, per_piece * rows), 1) // rows
    )

    def within(piece):
        at = columns(piece)
        inputs = x_ref[:, at]
        picks = turned_head == head_of_lane + piece * per_piece
        token_side = dot(turned, jnp.where(picks, 1.0, 0.0).astype(BF16), NN)
        line = jnp.concatenate(
            [cum_ref[pl.ds(piece * per_piece + n, 1), :] for n in range(per_piece)], axis=1
        )
        decay = jnp.exp2(jnp.where(wide_lower, token_side - line, -1e30))
        low = (decay * wide_products).astype(BF16)
        for n in range(per_piece):
            decays[piece * per_piece + n] = decay[:, n * rows : (n + 1) * rows]
            weights[piece * per_piece + n] = low[:, n * rows : (n + 1) * rows]
        alone = jnp.concatenate([inputs * mask for mask in head_masks], axis=0)
        mixer_out[:, at] = dot(low, alone, NN)

    def within_chunk(j):
        def two(n):
            within(j * PLANE + 2 * n)
            within(j * PLANE + 2 * n + 1)

        loop(0, PLANE // 2, two)

    def from_far(kind, distance):
        def one(plane):
            block = plane * PLANE + place
            landed(kind, 0, block)
            chip_relay(kind, block).start()
            core_relay(kind, block).start()

        at_distance(distance, one)

    chip_place = place + 2 - 4 * chip
    core_place = place + 1 - 2 * core

    def from_chip(kind, distance):
        def one(plane):
            block = plane * PLANE + chip_place
            landed(kind, 1, block)
            core_relay(kind, block).start()

        if distance:
            at_distance(distance, one)
        else:
            one(far)

    def total_here(other):
        arrived(totals.at[other], TOTAL, other, core_peer)

    loop(0, outer, own_chunk)
    within_chunk(0)
    total_here(core_place)
    loop(0, outer, ahead_scan.join)
    from_far(keys_kind, 1)
    from_chip(keys_kind, 0)
    from_far(keys_kind, 2)
    total_here(chip_place)
    total_here(3 - place)
    from_far(keys_kind, 3)
    from_far(values_kind, 1)
    from_chip(values_kind, 0)
    within_chunk(1)
    forward_chain(0, 0, 1)
    from_far(values_kind, 2)
    from_chip(keys_kind, 1)
    within_chunk(2)
    forward_chain(0, 1, 2)
    from_far(values_kind, 3)
    from_chip(keys_kind, 2)
    within_chunk(3)
    forward_chain(0, 2, 3)
    forward_chain(1, 0, 1)
    from_chip(keys_kind, 3)
    from_chip(values_kind, 1)
    forward_chain(0, 3, 4)
    forward_chain(1, 1, 2)

    def all_here(kind):
        def one(step):
            for at in (core_place, 3 - place):
                landed(kind, 2, far_device(step, at))

        loop(0, outer, one)

    loads[6].wait()
    loads[7].wait()
    all_here(keys_kind)

    key_count = size * width
    query_count = heads * width
    key_index = lax.broadcasted_iota(jnp.int32, (key_count, query_count), 0)
    query_index = lax.broadcasted_iota(jnp.int32, (key_count, query_count), 1)
    key_place = lax.rem(key_index, width) * size + key_index // width
    query_place = lax.rem(query_index, width) * size + me
    visible = query_place >= key_place
    per_block = width // per_partner

    def held_at(which_core, which_chip, plane):
        return (2 * which_core + which_chip) * outer + plane

    def rows_copy(peer):
        return copy_to(rows_out.at[peer], rows_in.at[me], QUERY_ROWS, peer, me, peer)

    def grad_core_copy(which, plane):
        return copy_to(
            keys_out.at[held_at(1 - core, which, plane)],
            keys_core.at[which, plane],
            GRAD_CORE,
            which * outer + plane,
            which * outer + plane,
            core_peer,
        )

    def grad_chip_copy(plane):
        return copy_to(
            keys_chip_out.at[plane], keys_chip.at[plane], GRAD_CHIP, plane, plane, chip_peer
        )

    def grad_outer_copy(plane):
        return copy_to(
            keys_outer_out.at[plane],
            keys_outer.at[far],
            GRAD_OUTER,
            plane,
            far,
            plane * PLANE + place,
        )

    def joined(which, plane):
        arrived(keys_core.at[which, plane], GRAD_CORE, which * outer + plane, core_peer)
        return keys_out[held_at(core, which, plane)].astype(F32) + keys_core[
            which, plane
        ].astype(F32)

    def send_plane(plane, query_rows):
        for at in range(PLANE):
            target = plane * PLANE + at
            part = slice(at * per_partner, (at + 1) * per_partner)
            rows_out[target] = (
                query_rows[:, part, :].reshape(heads * per_partner, head_dim).astype(BF16)
            )
            held = ((at % 2) * 2 + at // 2) * outer + plane
            keys_out[held, :, :head_dim] = (
                (key_acc[plane, :, part, :].reshape(rows, head_dim) * scale).astype(BF16)
            )
            keys_out[held, :, head_dim:] = (
                value_acc[plane, :, part, :].reshape(rows, head_dim).astype(BF16)
            )
        grad_core_copy(1 - chip, plane).start()
        grad_core_copy(chip, plane).start()

    def send_rows(plane):
        def one(at):
            target = plane * PLANE + at

            @pl.when(target == me)
            def _():
                rows_in[target] = rows_out[target]

            @pl.when(target != me)
            def _():
                rows_copy(target).start()

        loop(0, PLANE, one)

    def grads_to_chip(plane):
        keys_chip_out[plane] = joined(1 - chip, plane).astype(BF16)
        grad_chip_copy(plane).start()

    def grads_to_plane(plane):
        near = joined(chip, plane)
        arrived(keys_chip.at[plane], GRAD_CHIP, plane, chip_peer)
        low = (near + keys_chip[plane].astype(F32)).astype(BF16)

        @pl.when(plane == far)
        def _():
            keys_outer[far] = low

        @pl.when(plane != far)
        def _():
            keys_outer_out[plane] = low
            grad_outer_copy(plane).start()

    last = blocks - 1
    point = 0
    events = {
        1: [
            lambda: forward_chain(1, 2, 3),
            lambda: forward_chain(2, 0, 1),
            lambda: from_chip(values_kind, 2),
            lambda: from_chip(values_kind, 3),
            lambda: all_here(values_kind),
        ],
        2: [lambda: forward_chain(1, 3, 4), lambda: forward_chain(2, 1, 2)],
        3: [lambda: forward_chain(2, 2, 3), lambda: forward_chain(3, 0, 1)],
        4: [lambda: forward_chain(2, 3, 4), lambda: forward_chain(3, 1, 2), lambda: grads_to_chip(3)],
        5: [lambda: forward_chain(3, 2, 3), lambda: send_rows(3)],
        6: [lambda: forward_chain(3, 3, 4)],
        7: [lambda: send_rows(2), lambda: grads_to_chip(2), lambda: grads_to_plane(3)],
        10: [lambda: send_rows(1), lambda: grads_to_chip(1), lambda: grads_to_plane(2)],
        12: [lambda: send_rows(0), lambda: grads_to_chip(0), lambda: grads_to_plane(1)],
    }

    def reach():
        nonlocal point
        point += 1
        for event in events.get(point, ()):
            event()

    for block in range(blocks - 1, -1, -1):
        own_span = slice(block * width, (block + 1) * width)
        own_queries = jnp.concatenate(
            [q_ref[own_span, h * head_dim : (h + 1) * head_dim] for h in range(heads)], axis=0
        )
        own_grads = jnp.concatenate(
            [do_ref[own_span, h * head_dim : (h + 1) * head_dim] for h in range(heads)], axis=0
        )
        highest = None
        for other in range(block + 1):
            span_k = slice(other * width, (other + 1) * width)
            key_block = kbuf[:, span_k, :].reshape(key_count, head_dim)
            scores = dot(key_block, own_queries, NT)
            if other == block:
                scores = jnp.where(visible, scores, -1e30)
            exps[other] = scores
            top = jnp.max(scores, axis=0, keepdims=True)
            highest = top if highest is None else jnp.maximum(highest, top)
        reach()
        total = jnp.zeros((1, query_count), F32)
        delta = jnp.zeros((1, query_count), F32)
        for other in range(block + 1):
            span_k = slice(other * width, (other + 1) * width)
            value_block = vbuf[:, span_k, :].reshape(key_count, head_dim)
            prob_grad = dot(value_block, own_grads, NT)
            raised = jnp.exp2((exps[other] - highest) * (scale * LOG2E))
            total = total + jnp.sum(raised, axis=0, keepdims=True)
            delta = delta + jnp.sum(raised * prob_grad, axis=0, keepdims=True)
            exps[other] = raised
            prob_grads[other] = prob_grad
        reach()
        inverse = 1.0 / total
        delta = delta * inverse
        query_grad = jnp.zeros((head_dim, query_count), F32)
        for other in range(block + 1):
            span_k = slice(other * width, (other + 1) * width)
            key_block = kbuf[:, span_k, :].reshape(key_count, head_dim)
            probs = exps[other] * inverse
            score_grad = (probs * (prob_grads[other] - delta)).astype(BF16)
            query_grad = query_grad + dot(key_block, score_grad, TN)
            more_keys = dot(score_grad, own_queries, NN).reshape(size, width, head_dim)
            more_values = dot(probs.astype(BF16), own_grads, NN).reshape(size, width, head_dim)
            if block == last:
                key_acc[other] = more_keys
                value_acc[other] = more_values
            else:
                key_acc[other] += more_keys
                value_acc[other] += more_values
        send_plane(block, (query_grad * scale).T.reshape(heads, width, head_dim))
        reach()

    loop(0, outer, ahead_scan.hand_back_near)
    loop(0, outer, ahead_scan.hand_back_far)
    grads_to_plane(0)

    def carry_in(j):
        ahead_scan.results_here(j)
        at = chunk_columns(j)
        mixer_out[:, at] += grown[:, at] * dot(read_ref[...], ahead_scan.results(j), NN)

    loop(0, outer, carry_in)

    each_peer(lambda peer: arrived(rows_in.at[peer], QUERY_ROWS, peer, peer))

    def outer_here(step):
        other = lax.rem(far + step, outer)
        arrived(keys_outer.at[other], GRAD_OUTER, other, core_peer)

    loop(1, outer, outer_here)
    key_rows = keys_outer[0].astype(F32)
    for source in range(1, outer):
        key_rows = key_rows + keys_outer[source].astype(F32)
    shaped = rows_in[...].astype(F32).reshape(size, heads, per_partner, head_dim)
    grads = jnp.concatenate(
        [shaped[:, h].reshape(rows, head_dim).astype(BF16) for h in range(heads)]
        + [key_rows.astype(BF16)],
        axis=1,
    )
    token = lax.broadcasted_iota(jnp.int32, (rows, rows), 0)
    held_row = lax.broadcasted_iota(jnp.int32, (rows, rows), 1)
    order = (lax.rem(held_row, per_partner) * size + held_row // per_partner) == token
    grads = dot(jnp.where(order, 1.0, 0.0).astype(BF16), grads, NN).astype(BF16)
    loads[8].wait()
    loads[9].wait()
    loads[10].wait()

    def statistics(j, carry):
        squares, crosses = carry
        down = pl.ds(pl.multiple_of(j * span, span), span)
        rounded_all = dot(grads, weight[down, :], NT)
        for n in range(PLANE):
            at = columns(j * PLANE + n)
            rounded = rounded_all[:, n * LANES : (n + 1) * LANES].astype(BF16).astype(F32)
            scaled = gain_ref[:, at] * rounded
            mixed[:, at] = scaled
            gate = gate_ref[:, at].astype(F32)
            gated = mixer_out[:, at] * (gate * jax.nn.sigmoid(gate))
            squares = squares + gated * gated
            crosses = crosses + scaled * gated
        return (squares, crosses)

    empty = jnp.zeros((rows, LANES), F32)
    squares, crosses = lax.fori_loop(0, outer, statistics, (empty, empty))
    mean_square = jnp.sum(squares, axis=1, keepdims=True) / channels
    mean_cross = jnp.sum(crosses, axis=1, keepdims=True) / channels
    inverse_root = 1.0 / jnp.sqrt(mean_square + EPSILON)
    cross_factor = mean_cross * (inverse_root * inverse_root * inverse_root)

    def gate_chunk(j):
        for n in range(PLANE):
            at = columns(j * PLANE + n)
            gate = gate_ref[:, at].astype(F32)
            sigmoid = jax.nn.sigmoid(gate)
            active = gate * sigmoid
            out = mixer_out[:, at]
            gated_grad = mixed[:, at] * inverse_root - out * active * cross_factor
            ggrad_ref[:, at] = gated_grad * out * sigmoid * (1.0 + gate * (1.0 - sigmoid))
            low = (gated_grad * active).astype(BF16)
            out_grad[:, at] = low
            grown_grad[:, at] = (low.astype(F32) * grown[:, at]).astype(BF16)
        back_scan.store_own(j, dot(read_turned[...], grown_grad[:, chunk_columns(j)], NN))
        back_scan.send_core(j)

    def gate_step(j):
        gate_chunk(j)
        pl.when(j >= 1)(lambda: back_scan.join(j - 1))

    loop(0, outer, gate_step)
    back_scan.join(outer - 1)

    pair_sum[...] = jnp.zeros((rows, rows), F32)
    rgrad_ref[...] = jnp.zeros((rows, nstate), F32)
    wgrad_ref[...] = jnp.zeros((rows, nstate), F32)

    def grads_within(j):
        pairs = pair_sum[...]
        for n in range(PLANE):
            piece = j * PLANE + n
            at = columns(piece)
            grad_piece = out_grad[:, at]
            alone = jnp.concatenate([grad_piece * mask for mask in head_masks], axis=0)
            those = pl.ds(piece * per_piece, per_piece)
            igrad_ref[:, at] = dot(weights[those].reshape(per_piece * rows, rows), alone, TN)
            products_here = dot(alone, x_ref[:, at], NT)
            for h in range(per_piece):
                pairs = (
                    pairs
                    + decays[piece * per_piece + h] * products_here[h * rows : (h + 1) * rows]
                )
        pair_sum[...] = pairs
        rgrad_ref[...] += dot(grown_grad[:, chunk_columns(j)], ahead_scan.results(j), NT)

    def finish(j):
        back_scan.results_here(j)
        at = chunk_columns(j)
        carried = back_scan.results(j)
        igrad_ref[:, at] += remain[:, at] * dot(write_ref[...], carried, NN)
        wgrad_ref[...] += dot(remain_input[:, at], carried, NT)

    from_last = outer - 1 - far
    delay = jnp.where(from_last == 0, outer, 0)

    def back_point(step):
        j = step - 2 * from_last
        pl.when((j >= 0) & (j < outer))(lambda: back_scan.chain_on(j))
        back = j - delay

        @pl.when((back >= 0) & (back < outer))
        def _():
            back_scan.chain_back(back)
            back_scan.hand_back_near(back)

        pl.when((back >= 2) & (back <= outer + 1))(lambda: back_scan.hand_back_far(back - 2))
        pl.when((back >= 4) & (back <= outer + 3))(lambda: finish(back - 4))

    def within_point(step):
        grads_within(step)
        back_point(step)

    loop(0, outer, within_point)
    pairs_low = pair_sum[...].astype(BF16)
    rgrad_ref[...] += dot(pairs_low, write_ref[...], NN)
    wgrad_ref[...] += dot(pairs_low, read_ref[...], TN)
    loop(outer, 3 * outer + 2, back_point)

    def relays_sent(step):
        for kind in (keys_kind, values_kind):
            block = far_device(step, place)
            chip_relay(kind, block).wait_send()
            core_relay(kind, block).wait_send()
            core_relay(kind, far_device(step, chip_place)).wait_send()

    for kind in (keys_kind, values_kind):
        for distance in range(1, outer):
            at_distance(distance, lambda plane: outer_relay(kind, plane).wait_send())
    loop(0, outer, relays_sent)
    loop(1, PLANE, lambda step: total_copy(step).wait_send())
    each_peer(lambda peer: rows_copy(peer).wait_send())

    def grads_sent(plane):
        grad_core_copy(0, plane).wait_send()
        grad_core_copy(1, plane).wait_send()
        grad_chip_copy(plane).wait_send()
        pl.when(plane != far)(lambda: grad_outer_copy(plane).wait_send())

    loop(0, outer, grads_sent)
    ahead_scan.sent()
    back_scan.sent()


def hand_over(*refs):
    done = refs[-1]
    copies = [
        pltpu.make_async_copy(refs[n], refs[n + 4], done.at[n]) for n in range(4)
    ]
    for copy in copies:
        copy.start()
    for copy in copies:
        copy.wait()


def fused_body(
    queries,
    keys,
    values,
    d_out,
    mixer_input,
    gate_input,
    state_write,
    state_read,
    log_decay,
    norm_gain,
    project_weight,
):
    arguments = (
        queries,
        keys,
        values,
        d_out,
        mixer_input,
        gate_input,
        state_write,
        state_read,
        log_decay,
        norm_gain,
        project_weight,
    )
    size = lax.axis_size("ctx")
    rows, head_dim = keys.shape
    heads = queries.shape[1] // head_dim
    channels = mixer_input.shape[1]
    mheads = log_decay.shape[1]
    mdim = channels // mheads
    nstate = state_write.shape[1]
    blocks = 4
    width = rows // blocks
    per_partner = rows // size
    if channels != size * LANES or LANES % mdim or per_partner % 8 or width % per_partner or size != blocks * PLANE or blocks != 4:
        return body(*arguments)
    per_piece = LANES // mdim
    key_count = size * width
    query_count = heads * width
    outer = size // PLANE
    pieces = pltpu.VMEM((size, nstate, LANES), BF16)
    fewer = pltpu.VMEM((outer, nstate, LANES), BF16)
    scan_buffers = [pieces] * 4 + [fewer] * 2 + [pieces] * 4
    scratch = [
        pltpu.VMEM(queries.shape, BF16),
        pltpu.VMEM(d_out.shape, BF16),
        pltpu.VMEM(mixer_input.shape, BF16),
        pltpu.VMEM(gate_input.shape, BF16),
        pltpu.VMEM(state_write.shape, BF16),
        pltpu.VMEM(state_read.shape, BF16),
        pltpu.VMEM((mheads, rows), F32),
        pltpu.VMEM((1, channels), F32),
        pltpu.VMEM((mheads, rows), F32),
        pltpu.VMEM((nstate, rows), BF16),
        pltpu.VMEM((nstate, rows), BF16),
        pltpu.VMEM((size, rows, head_dim), BF16),
        pltpu.VMEM((size, rows, head_dim), BF16),
        pltpu.VMEM((1, channels), F32),
        pltpu.VMEM((PLANE, 1, channels), F32),
        pltpu.VMEM((size, heads * per_partner, head_dim), BF16),
        pltpu.VMEM((size, heads * per_partner, head_dim), BF16),
        pltpu.VMEM((size, rows, 2 * head_dim), BF16),
        pltpu.VMEM((2, outer, rows, 2 * head_dim), BF16),
        pltpu.VMEM((outer, rows, 2 * head_dim), BF16),
        pltpu.VMEM((outer, rows, 2 * head_dim), BF16),
        pltpu.VMEM((outer, rows, 2 * head_dim), BF16),
        pltpu.VMEM((outer, rows, 2 * head_dim), BF16),
        *scan_buffers,
        *scan_buffers,
        pltpu.VMEM((blocks, key_count, query_count), F32),
        pltpu.VMEM((blocks, key_count, query_count), F32),
        pltpu.VMEM((blocks, size, width, head_dim), F32),
        pltpu.VMEM((blocks, size, width, head_dim), F32),
        pltpu.VMEM((mheads, rows, rows), F32),
        pltpu.VMEM((mheads, rows, rows), BF16),
        pltpu.VMEM((rows, channels), F32),
        pltpu.VMEM((rows, channels), F32),
        pltpu.VMEM((rows, channels), F32),
        pltpu.VMEM((rows, channels), F32),
        pltpu.VMEM((rows, channels), BF16),
        pltpu.VMEM((rows, channels), BF16),
        pltpu.VMEM((rows, channels), BF16),
        pltpu.VMEM((rows, rows), F32),
        pltpu.VMEM(project_weight.shape, project_weight.dtype),
        pltpu.SemaphoreType.DMA((11,)),
        pltpu.SemaphoreType.DMA((PHASES, size)),
        pltpu.SemaphoreType.DMA((PHASES, size)),
    ]
    vmem = pl.BlockSpec(memory_space=pltpu.VMEM)
    results = pl.pallas_call(
        functools.partial(fused_kernel, size, mdim),
        out_shape=(
            pltpu.VMEM((rows, channels), F32),
            pltpu.VMEM((rows, channels), F32),
            pltpu.VMEM((rows, nstate), F32),
            pltpu.VMEM((rows, nstate), F32),
        ),
        in_specs=[pl.BlockSpec(memory_space=pl.ANY)] * 11,
        out_specs=(vmem,) * 4,
        scratch_shapes=scratch,
        compiler_params=pltpu.CompilerParams(
            collective_id=0, has_side_effects=True, vmem_limit_bytes=56 * 1024 * 1024
        ),
    )(
        queries,
        keys,
        values,
        d_out,
        mixer_input,
        gate_input,
        state_write,
        state_read,
        log_decay.T,
        norm_gain[None, :],
        project_weight,
    )
    anywhere = pl.BlockSpec(memory_space=pl.ANY)
    return pl.pallas_call(
        hand_over,
        out_shape=tuple(jax.ShapeDtypeStruct(r.shape, r.dtype) for r in results),
        in_specs=[anywhere] * 4,
        out_specs=(anywhere,) * 4,
        scratch_shapes=[pltpu.SemaphoreType.DMA((4,))],
    )(*[pltpu.with_memory_space_constraint(r, pltpu.VMEM) for r in results])


def solution(mesh):
    placed = (
        P("ctx", "groups"),
        P("ctx", "groups"),
        P("ctx", "groups"),
        P("ctx", "groups"),
        P("ctx", "groups"),
        P("ctx", "groups"),
        P("ctx", "groups"),
        P("ctx", "groups"),
        P("ctx", "groups"),
        P("groups"),
        P(None, "groups"),
    )
    return jax.shard_map(
        fused_body,
        mesh=mesh,
        in_specs=placed,
        out_specs=(P("ctx", "groups"), P("ctx", "groups"), P("ctx", "groups"), P("ctx", "groups")),
        check_vma=False,
    )
```
